32 devices in a mesh: dp: 4 (over y, x), ctx: 8 (over z, core).
Axes of the slice: x: 2, y: 2, z: 4, core: 2. Of those that a mesh axis runs over, the one named last changes fastest.
Arguments:
- inputs: bfloat16 [4, 2048, 4096], P('dp', 'ctx'), may hold values from -6 to 6
- query_weight: bfloat16 [4096, 128], P('dp'), may hold values from -0.09375 to 0.09375
- key_weight: bfloat16 [4096, 128], P('dp'), may hold values from -0.09375 to 0.09375
- value_weight: bfloat16 [4096, 2048], P('dp'), may hold values from -0.09375 to 0.09375
- lambda_weight: bfloat16 [4096, 320], P('dp'), may hold values from -0.09375 to 0.09375
- log_decay: float32 [4, 2048, 16], P('dp', 'ctx'), may hold values from -1 to 0, as said below
- norm_gain: float32 [2048], replicated, may hold values from 0.5 to 1.5
Outputs:
- outputs: bfloat16 [4, 2048, 2048], P('dp', 'ctx')
The draws below stay inside these ranges and needn't reach their ends.
Inputs may be any that keep to these rules, and one draw needn't show every extreme that they name: `log_decay`: entries are not positive.
All inputs are finite; a program needn't handle non-finite values.
Results may differ from the reference program's by a relative error of at most 0.0072.
Values may be sent and summed in bfloat16 or wider, within the bound.
A program may use at most 128 MiB of HBM per device.

```python
import math
import jax
import jax.numpy as jnp
from jax import lax

D = 4096
HEADS = 16
HEAD = 128
STATE = 128
LAMBDAS = 20
TOK_DEV = 256
SEQUENCE_TOTAL = 4
SEQUENCE_SPAN = 2048
N_CTX = 8


def draw_log_decay(key, part):
    key_kind = jax.random.fold_in(key, 11)
    key_slow = jax.random.fold_in(key, 12)
    key_pick = jax.random.fold_in(key, 13)
    key_token = jax.random.fold_in(key, 14)
    key_block = jax.random.fold_in(key, 15)
    key_spurt = jax.random.fold_in(key, 16)
    key_keep = jax.random.fold_in(key, 17)
    key_width = jax.random.fold_in(key, 18)
    key_offset = jax.random.fold_in(key, 19)
    key_mass = jax.random.fold_in(key, 20)
    block_count = SEQUENCE_SPAN // TOK_DEV
    mixed_count = max(HEADS // 2, 1)
    fast_share = 0.5
    order = jax.random.permutation(key_kind, HEADS)
    mixed_head = order < mixed_count
    slow_rate = jnp.exp(jax.random.uniform(key_slow, (HEADS,), jnp.float32, math.log(0.05), math.log(0.4))) / SEQUENCE_SPAN
    block_shape = (SEQUENCE_TOTAL, block_count, 1, HEADS)
    fast_block = jnp.logical_and(jax.random.uniform(key_pick, block_shape, jnp.float32) < fast_share, mixed_head[None, None, None, :])
    token = jax.random.uniform(key_token, (SEQUENCE_TOTAL, block_count, TOK_DEV, HEADS), jnp.float32, 0.5, 2.0)
    blocks = jnp.exp(jax.random.uniform(key_block, block_shape, jnp.float32, -0.7, 0.7))
    slow_part = token * blocks * slow_rate[None, None, None, :]
    width = jax.random.randint(key_width, block_shape, max(TOK_DEV // 8, 1), TOK_DEV + 1)
    offset = jax.random.randint(key_offset, block_shape, 0, TOK_DEV) % (TOK_DEV - width + 1)
    position_in = jnp.arange(TOK_DEV, dtype=jnp.int32)[None, None, :, None]
    inside = jnp.logical_and(position_in >= offset, position_in < offset + width)
    mass = jnp.exp(jax.random.uniform(key_mass, block_shape, jnp.float32, math.log(8.0), math.log(16.0)))
    fast_part = jnp.where(inside, jnp.minimum(mass / width.astype(jnp.float32) * token, 1.0), slow_part)
    elementwise_rate = jnp.where(fast_block, fast_part, slow_part).reshape(SEQUENCE_TOTAL, SEQUENCE_SPAN, HEADS)
    spurt_index = jax.random.randint(key_spurt, (SEQUENCE_TOTAL, 3), 0, SEQUENCE_SPAN)
    token_place = jnp.arange(SEQUENCE_SPAN, dtype=jnp.int32)
    spurt_mask = jnp.any(token_place[None, :, None] == spurt_index[:, None, :], axis=-1)
    kept_entries = jax.random.uniform(key_keep, (SEQUENCE_TOTAL, SEQUENCE_SPAN, 1), jnp.float32, 0.55, 0.8)
    spurt_portion = jnp.where(spurt_mask[:, :, None], jnp.log(kept_entries), 0.0)
    return jnp.maximum(spurt_portion - elementwise_rate, -1.0).astype(jnp.float32)


def level_of(stream_key, extent, cuts, low, high):
    factor_of = 1.0
    for axis_at, shards_of in cuts:
        steps = jax.random.uniform(jax.random.fold_in(jax.random.fold_in(stream_key, 6), axis_at), (shards_of,), jnp.float32, low / len(cuts), high / len(cuts))
        factor_of = factor_of * jnp.repeat(jnp.exp(steps), extent[axis_at] // shards_of).reshape((-1,) + (1,) * (len(extent) - 1 - axis_at))
    return factor_of


def scatter_about(stream_key, shape, deviation, most, shards=(), held_as=jnp.bfloat16):
    drawn = jax.random.normal(stream_key, shape, jnp.float32) * deviation
    if len(shards) > 0:
        drawn = level_of(stream_key, shape, shards, -0.22, 0.18) * drawn
    return jnp.clip(drawn, min=-most, max=most).astype(held_as)


def setup_inputs(seed: int = 0) -> dict:
    keys = jax.random.split(jax.random.key(seed), 8)
    return {
        "inputs": scatter_about(keys[0], (SEQUENCE_TOTAL, SEQUENCE_SPAN, D), 1.0, 6.0, ((0, 4), (1, 8))),
        "query_weight": scatter_about(keys[1], (D, STATE), D ** -0.5, 0.09375, ((0, 4),)),
        "key_weight": scatter_about(keys[2], (D, STATE), D ** -0.5, 0.09375, ((0, 4),)),
        "value_weight": scatter_about(keys[3], (D, HEADS * HEAD), D ** -0.5, 0.09375, ((0, 4),)),
        "lambda_weight": scatter_about(keys[4], (D, HEADS * LAMBDAS), D ** -0.5, 0.09375, ((0, 4),)),
        "log_decay": draw_log_decay(jax.random.fold_in(keys[7], 71), 0),
        "norm_gain": jnp.clip(1.0 + 0.1 * jax.random.normal(keys[6], (HEADS * HEAD,), jnp.float32), 0.5, 1.5),
    }


HIGHEST = lax.Precision.HIGHEST

def level_masks(length):
    depth = length.bit_length() - 1
    token_place = jnp.arange(length, dtype=jnp.int32)
    differ = jnp.bitwise_xor(token_place[:, None], token_place[None, :])
    level = jnp.zeros((length, length), jnp.int32)
    for power in range(depth):
        level = level + (differ >= 1 << power).astype(jnp.int32)
    levels = jnp.arange(depth + 1, dtype=jnp.int32)
    return (level[None, :, :] == levels[:, None, None]).astype(jnp.float32)

def block_terms(query_rows, key_rows, value_rows, lambdas, log_decay, masks):
    length, heads = log_decay.shape
    state_dim = query_rows.shape[1]
    head_dim = value_rows.shape[1] // heads
    inner = masks.shape[0]
    weights_all = lambdas.reshape(length, heads, -1)
    cumulative = jnp.cumsum(log_decay, axis=0)
    scores = jnp.dot(query_rows, key_rows.T, preferred_element_type=jnp.float32) / math.sqrt(state_dim)
    level_weight = jnp.einsum('lts,thl->hts', masks, weights_all[:, :, :inner], precision=HIGHEST)
    token_place = jnp.arange(length, dtype=jnp.int32)
    causal = token_place[:, None] >= token_place[None, :]
    spread = jnp.transpose(cumulative)
    distance = spread[:, :, None] - spread[:, None, :]
    decay = jnp.exp(jnp.where(causal[None], distance, -jnp.inf))
    mix = (level_weight * decay * scores[None]).astype(jnp.bfloat16)
    values = value_rows.reshape(length, heads, head_dim)
    near = jnp.einsum('hts,shd->thd', mix.astype(jnp.float32), values.astype(jnp.float32), precision=HIGHEST)
    remain = jnp.exp(cumulative[-1][None, :] - cumulative)
    keyed = (key_rows.astype(jnp.float32)[:, None, :] * remain[:, :, None]).astype(jnp.bfloat16)
    state = jnp.einsum('chs,chd->hsd', keyed.astype(jnp.float32), values.astype(jnp.float32), precision=HIGHEST)
    total = jnp.exp(cumulative[-1])
    return (near, state, total, cumulative, weights_all)

def finish(mixed, norm_gain):
    heads = mixed.shape[-2]
    mean_square = lax.optimization_barrier(jnp.mean(mixed * mixed, axis=-1, keepdims=True))
    return (mixed * lax.rsqrt(mean_square + 1e-05) * norm_gain.reshape(heads, -1)).astype(jnp.bfloat16)

def reference(inputs, query_weight, key_weight, value_weight, lambda_weight, log_decay, norm_gain):
    bits = N_CTX.bit_length() - 1
    masks = level_masks(TOK_DEV)
    inner = masks.shape[0]
    scale = 1.0 / math.sqrt(STATE)

    def one_sequence(pair):
        sequence, decays = pair
        query_rows = jnp.dot(sequence, query_weight, preferred_element_type=jnp.float32).astype(jnp.bfloat16)
        key_rows = jnp.dot(sequence, key_weight, preferred_element_type=jnp.float32).astype(jnp.bfloat16)
        value_rows = jnp.dot(sequence, value_weight, preferred_element_type=jnp.float32).astype(jnp.bfloat16)
        lambdas = jax.nn.softplus(jnp.dot(sequence, lambda_weight, preferred_element_type=jnp.float32))

        def per_block(pieces):
            return block_terms(pieces[0], pieces[1], pieces[2], pieces[3], pieces[4], masks)
        near, state, total, cumulative, weights_all = lax.map(per_block, (query_rows.reshape(N_CTX, TOK_DEV, -1), key_rows.reshape(N_CTX, TOK_DEV, -1), value_rows.reshape(N_CTX, TOK_DEV, -1), lambdas.reshape(N_CTX, TOK_DEV, -1), decays.reshape(N_CTX, TOK_DEV, -1)))
        block_index = jnp.arange(N_CTX, dtype=jnp.int32)
        block_state = state
        block_total = total
        carry_decay = jnp.ones_like(total)
        query_blocks = query_rows.reshape(N_CTX, TOK_DEV, -1).astype(jnp.float32)
        mixed = near
        for level_bit in range(bits):
            partner = jnp.bitwise_xor(block_index, jnp.int32(1 << level_bit))
            other_state = block_state[partner]
            other_total = block_total[partner]
            upper = (block_index >> level_bit & 1).astype(jnp.float32)
            carried = (carry_decay[:, :, None, None] * other_state).astype(jnp.bfloat16)
            reach = jnp.einsum('jts,jhsd->jthd', query_blocks, carried.astype(jnp.float32), precision=HIGHEST)
            factor = weights_all[:, :, :, inner + level_bit] * jnp.exp(cumulative) * (scale * upper[:, None, None])
            mixed = mixed + factor[..., None] * reach
            if level_bit + 1 < bits:
                flag = upper[:, None, None, None] > 0
                block_state = jnp.where(flag, block_total[:, :, None, None] * other_state + block_state, other_total[:, :, None, None] * block_state + other_state)
                carry_decay = jnp.where(upper[:, None] > 0, other_total * carry_decay, carry_decay)
                block_total = block_total * other_total
        return finish(mixed, norm_gain).reshape(SEQUENCE_SPAN, -1)
    return lax.map(one_sequence, (inputs, log_decay))
```

```python
import functools
import math

import jax
import jax.numpy as jnp
from jax import lax
from jax.experimental import pallas as pl
from jax.experimental.pallas import tpu as pltpu
from jax.sharding import PartitionSpec as P

HIGHEST = lax.Precision.HIGHEST
MESH = pl.DeviceIdType.MESH
VMEM_LIMIT = 60 * 1024 * 1024

PIECES = 2
AHEAD = 3
SHARE = 5 / 16
LANES = 128


def flipped(index, mask):
    out = index
    for power in range(mask.bit_length()):
        if mask >> power & 1:
            step = 1 << power
            out = out + step - 2 * step * ((index // step) % 2)
    return out


def fused_kernel(levels, x_ref, q_ref, k_ref, lam_t_ref, v_ref, decay_ref, gain_ref, out_ref,
                 xs, dec, big_q, big_k, big_l, big_v, qk, lam, val, score, cum_rows, cum_cols,
                 grow, reach_grow, remain, logs, coef, state, sent, got, mixed, result,
                 load_sem, swap_send, swap_recv, own_send, own_recv, relay_send, relay_recv,
                 z_send, z_recv, core_send, core_recv, log_send, log_recv, st_send, st_recv,
                 out_sem, give_send, give_recv):
    f32, bf16 = jnp.float32, jnp.bfloat16
    count = lax.axis_size("ctx")
    chips = count // 2
    bits = count.bit_length() - 1
    dp = lax.axis_index("dp")
    ctx = lax.axis_index("ctx")
    x_at, y_at = dp % 2, dp // 2
    core = ctx % 2
    side = (ctx // 2) % 2
    length = x_ref.shape[0]
    depth, wide = v_ref.shape
    nh = decay_ref.shape[0] // 2
    lams = lam_t_ref.shape[0] // 2
    head_dim = wide // (2 * nh)
    state_dim = q_ref.shape[1]
    inner = length.bit_length()
    scale = 1.0 / math.sqrt(state_dim)
    to_x = {"dp": y_at * 2 + (1 - x_at)}
    to_y = {"dp": (1 - y_at) * 2 + x_at}
    to_core = {"ctx": flipped(ctx, 1)}
    to_z = {"ctx": flipped(ctx, 2)}
    peers = [None] + [{"ctx": flipped(ctx, 2 * r)} for r in range(1, chips)]
    owners = (y_at * 2 + (1 - x_at), (1 - y_at) * 2 + x_at, (1 - y_at) * 2 + (1 - x_at), dp)
    started = []

    def remote(src, dst, out_sem_, in_sem, target):
        copy = pltpu.make_async_remote_copy(
            src_ref=src, dst_ref=dst, send_sem=out_sem_, recv_sem=in_sem,
            device_id=target, device_id_type=MESH)
        copy.start()
        started.append(copy)

    def await_at(spot, sem):
        pltpu.make_async_copy(spot, spot, sem).wait()

    barrier = pltpu.get_barrier_semaphore()
    greeted = [to_x, to_y, to_core] + peers[1:]
    for target in greeted:
        pl.semaphore_signal(barrier, inc=1, device_id=target, device_id_type=MESH)

    my_rows = pl.ds(pl.multiple_of(core * length, length), length)
    my_heads = pl.ds(pl.multiple_of(core * nh, nh), nh)
    their_heads = pl.ds(pl.multiple_of((1 - core) * nh, nh), nh)
    my_lams = pl.ds(pl.multiple_of(core * lams, 16), lams)
    my_cols = pl.ds(pl.multiple_of(core * nh * head_dim, LANES), nh * head_dim)

    def head_cols(h):
        return pl.ds(pl.multiple_of((core * nh + h) * head_dim, LANES), head_dim)

    local = [
        pltpu.make_async_copy(decay_ref.at[my_heads], dec.at[my_heads], load_sem.at[0]),
        pltpu.make_async_copy(x_ref, xs.at[my_rows], load_sem.at[1]),
        pltpu.make_async_copy(q_ref, big_q.at[3], load_sem.at[2]),
        pltpu.make_async_copy(k_ref, big_k.at[3], load_sem.at[3]),
        pltpu.make_async_copy(lam_t_ref.at[my_lams], big_l.at[3], load_sem.at[4]),
    ] + [pltpu.make_async_copy(v_ref.at[:, head_cols(h)], big_v.at[h, 3], load_sem.at[5 + h])
         for h in range(nh)]

    half = depth // 2
    pieces = [(q_ref, None, big_q, core * half, core * half, half),
              (k_ref, None, big_k, core * half, core * half, half),
              (lam_t_ref, None, big_l, core * lams, 0, lams)]
    part = depth // PIECES
    for h in range(nh):
        for p in range(PIECES):
            pieces.append((v_ref, head_cols(h), big_v.at[h], p * part, p * part, part))
    total = len(pieces)

    def shares(i):
        n = pieces[i][5]
        shared = int(n * SHARE / 16 + 0.5) * 16
        direct = n - shared
        first = (direct // 2 + 15) // 16 * 16
        return shared, direct, first

    def rows_at(base, start, size):
        return pl.ds(pl.multiple_of(base + start, 16), size)

    def send_own(i):
        src, cols, buf, src_base, base, n = pieces[i]
        shared, direct, first = shares(i)
        rows = rows_at(src_base, side * shared, direct)
        from_ = src.at[rows] if cols is None else src.at[rows, cols]
        for way, target in enumerate((to_x, to_y)):
            remote(from_, buf.at[way, rows_at(base, side * shared, direct)],
                   own_send.at[way, i], own_recv.at[way, i], target)

    def relay(i):
        src, cols, buf, src_base, base, n = pieces[i]
        shared, direct, first = shares(i)
        for way in range(2):
            await_at(buf.at[way, rows_at(base, side * shared, direct)], own_recv.at[way, i])
        for way, target, start, size in ((0, to_y, 0, first), (1, to_x, first, direct - first)):
            rows = rows_at(base, side * shared + start, size)
            remote(buf.at[way, rows], buf.at[2, rows], relay_send.at[way, i],
                   relay_recv.at[way, i], target)
        for way in range(2):
            pass_on(i, way)

    def pass_on(i, way):
        src, cols, buf, src_base, base, n = pieces[i]
        shared, direct, first = shares(i)
        rows = rows_at(base, side * direct, shared)
        remote(buf.at[way, rows], buf.at[way, rows], z_send.at[way, i], z_recv.at[way, i], to_z)

    def crossed(i):
        src, cols, buf, src_base, base, n = pieces[i]
        shared, direct, first = shares(i)
        for way, start, size in ((0, 0, first), (1, first, direct - first)):
            await_at(buf.at[2, rows_at(base, side * shared + start, size)], relay_recv.at[way, i])
        pass_on(i, 2)

    def shared_in(i):
        src, cols, buf, src_base, base, n = pieces[i]
        shared, direct, first = shares(i)
        for way in range(3):
            await_at(buf.at[way, rows_at(base, (1 - side) * direct, shared)], z_recv.at[way, i])
        if i < 2:
            rows = rows_at(base, 0, n)
            spot = buf.at[pl.ds(0, 3), rows]
            remote(spot, spot, core_send.at[i], core_recv.at[i], to_core)

    def own_part(way):
        return pl.ds(pl.multiple_of(owners[way] * depth, depth), depth)

    def gathered(weights, dims):
        acc = None
        for way in (3, 0, 1, 2):
            term = lax.dot_general(
                xs[:, own_part(way)], weights(way), dims, preferred_element_type=f32)
            acc = term if acc is None else acc + term
        return acc

    plain = (((1,), (0,)), ((), ()))
    turned = (((1,), (1,)), ((), ()))

    def task_qk():
        for i, buf in enumerate((big_q, big_k)):
            await_at(buf.at[pl.ds(0, 3), rows_at((1 - core) * half, 0, half)], core_recv.at[i])
        qk[:, :state_dim] = gathered(lambda way: big_q[way], plain).astype(bf16)
        qk[:, state_dim:] = gathered(lambda way: big_k[way], plain).astype(bf16)
        row = lax.broadcasted_iota(jnp.int32, (length, length), 0)
        col = lax.broadcasted_iota(jnp.int32, (length, length), 1)
        for blk in range(2):
            rows = slice(blk * length, (blk + 1) * length)
            full = lax.dot_general(
                qk[rows, :state_dim], qk[rows, state_dim:], turned, preferred_element_type=f32)
            score[blk] = jnp.where(row >= col, full * scale, 0.0)

    def task_lam():
        lam[...] = jax.nn.softplus(gathered(lambda way: big_l[way], turned))

    def task_sums():
        row = lax.broadcasted_iota(jnp.int32, (length, length), 0)
        col = lax.broadcasted_iota(jnp.int32, (length, length), 1)
        below = (row >= col).astype(f32)
        decays = dec[...]
        ones = jnp.ones((length, LANES), f32)
        sums = jnp.dot(decays, ones, precision=HIGHEST, preferred_element_type=f32)
        logs[0] = sums[:nh] + sums[nh:]
        coef[0, 0] = jnp.exp(sums[nh:])
        for r in range(1, chips):
            remote(logs.at[0], logs.at[r], log_send.at[r], log_recv.at[r], peers[r])
        cum_col = lax.dot_general(
            below, decays, turned, precision=HIGHEST, preferred_element_type=f32)
        cum_rows[...] = lax.dot_general(
            decays, below, turned, precision=HIGHEST, preferred_element_type=f32)
        moved = jnp.concatenate((jnp.zeros((nh, length), f32), decays[:nh]), axis=0)
        before = lax.dot_general(
            jnp.ones((length, length), f32), moved, turned, precision=HIGHEST,
            preferred_element_type=f32)
        cum_cols[...] = cum_col
        grow[...] = jnp.exp(cum_col) * scale
        reach_grow[...] = jnp.exp(cum_col + before) * scale
        remain[...] = jnp.exp(cum_col[length - 1:length] - cum_col)

    def task_coef():
        for r in range(1, chips):
            await_at(logs.at[r], log_recv.at[r])
        own_log = logs[0]
        carry_log = jnp.zeros_like(own_log)
        for b in range(1, bits):
            upper = ((ctx // (1 << b)) % 2).astype(f32)
            step = 1 << (b - 1)
            other = logs[step]
            for r in range(step + 1, 2 * step):
                other = other + logs[r]
            coef[b, 0] = jnp.exp(carry_log) * upper
            coef[b, 1] = jnp.where(upper > 0, 1.0, jnp.exp(other))
            coef[b, 2] = jnp.where(upper > 0, jnp.exp(own_log), 1.0)
            carry_log = carry_log + upper * other
            own_log = own_log + other

    def send_state(h, b):
        remote(sent.at[b, h], got.at[b, h], st_send.at[b, h], st_recv.at[b, h],
               peers[1 << (b - 1)])

    def task_head(h):
        val[h] = gathered(lambda way: big_v[h, way], plain).astype(bf16)
        blocks = []
        for blk in range(2):
            rows = slice(blk * length, (blk + 1) * length)
            at = blk * nh + h
            keyed = (qk[rows, state_dim:].astype(f32) * remain[:, at:at + 1]).astype(bf16)
            blocks.append(lax.dot_general(
                keyed, val[h, rows], (((0,), (0,)), ((), ())), preferred_element_type=f32))
        sent[0, h] = blocks[0].astype(bf16)
        if bits > 1:
            whole = coef[0, 0, h:h + 1] * blocks[0] + blocks[1]
            state[h] = whole
            sent[1, h] = whole.astype(bf16)
            send_state(h, 1)

    tile = 128
    tiles = length // tile

    def task_near(h, blk):
        trow = lax.broadcasted_iota(jnp.int32, (tile, tile), 0)
        tcol = lax.broadcasted_iota(jnp.int32, (tile, tile), 1)
        differ = jnp.bitwise_xor(trow, tcol)
        deep = tile.bit_length() - 1
        base = h * levels
        at_cum = blk * nh + h
        low = blk * length
        for ti in range(tiles):
            rows = slice(low + ti * tile, low + (ti + 1) * tile)
            here = slice(ti * tile, (ti + 1) * tile)
            acc = None
            for tj in range(ti + 1):
                cols = slice(tj * tile, (tj + 1) * tile)
                if ti == tj:
                    weight = jnp.broadcast_to(lam[rows, base:base + 1], (tile, tile))
                    for level in range(1, deep + 1):
                        at = base + level
                        weight = jnp.where(
                            differ >= 1 << (level - 1), lam[rows, at:at + 1], weight)
                else:
                    at = base + deep + (ti ^ tj).bit_length()
                    weight = lam[rows, at:at + 1]
                distance = cum_cols[here, at_cum:at_cum + 1] - cum_rows[at_cum:at_cum + 1, cols]
                decay = jnp.exp(jnp.minimum(distance, 0.0))
                mix = (weight * (decay * score[blk, here, cols])).astype(bf16)
                term = jnp.dot(
                    mix, val[h, low + tj * tile:low + (tj + 1) * tile],
                    preferred_element_type=f32)
                acc = term if acc is None else acc + term
            if blk == 1:
                reach = jnp.dot(qk[rows, :state_dim], sent[0, h], preferred_element_type=f32)
                at = base + inner
                acc = acc + lam[rows, at:at + 1] * grow[here, at_cum:at_cum + 1] * reach
            mixed[h, rows] = acc

    def far(h, b):
        carried = (coef[b, 0, h:h + 1] * got[b, h].astype(f32)).astype(bf16)
        reach = jnp.dot(qk[:, :state_dim], carried, preferred_element_type=f32)
        at = h * levels + inner + b
        grown = jnp.concatenate((reach_grow[:, h:h + 1], reach_grow[:, nh + h:nh + h + 1]), axis=0)
        return lam[:, at:at + 1] * grown * reach

    def task_merge(h, b):
        await_at(got.at[b, h], st_recv.at[b, h])
        block = coef[b, 1, h:h + 1] * state[h] + coef[b, 2, h:h + 1] * got[b, h].astype(f32)
        state[h] = block
        sent[b + 1, h] = block.astype(bf16)
        send_state(h, b + 1)
        mixed[h] += far(h, b)

    def task_finish(h):
        whole = mixed[h]
        if bits > 1:
            await_at(got.at[bits - 1, h], st_recv.at[bits - 1, h])
            whole = whole + far(h, bits - 1)
        mean_square = jnp.mean(whole * whole, axis=-1, keepdims=True)
        gain = gain_ref[:, head_cols(h)]
        result[h] = (whole * lax.rsqrt(mean_square + 1e-05) * gain).astype(bf16)
        remote(result.at[h, pl.ds(pl.multiple_of((1 - core) * length, length), length)],
               out_ref.at[:, head_cols(h)], give_send.at[h], give_recv.at[h], to_core)
        copy = pltpu.make_async_copy(
            result.at[h, my_rows], out_ref.at[:, head_cols(h)], out_sem.at[h])
        copy.start()
        return copy

    for copy in local:
        copy.start()
    pl.semaphore_wait(barrier, len(greeted))
    for i in range(AHEAD):
        send_own(i)
    remote(decay_ref.at[their_heads], dec.at[my_heads], swap_send.at[0], swap_recv.at[0], to_core)
    remote(x_ref, xs.at[my_rows], swap_send.at[1], swap_recv.at[1], to_core)
    local[0].wait()
    await_at(dec.at[their_heads], swap_recv.at[0])
    task_sums()
    for copy in local[1:]:
        copy.wait()
    await_at(xs.at[pl.ds(pl.multiple_of((1 - core) * length, length), length)], swap_recv.at[1])

    tasks = {}

    def plan(step, *what):
        tasks.setdefault(step, []).extend(what)

    lag = 2
    plan(lag + 1, task_coef)
    plan(lag + 2, task_qk, task_lam)
    outputs = []

    def finish(h):
        outputs.append(task_finish(h))

    for h in range(nh):
        done = 3 + (h + 1) * PIECES - 1 + lag
        plan(done, functools.partial(task_head, h), functools.partial(task_near, h, 0))
        after = done + (1 if PIECES > 1 else 0)
        plan(after, functools.partial(task_near, h, 1))
        plan(after, *[functools.partial(task_merge, h, b) for b in range(1, bits - 1)])
        if h > 0:
            plan(after, functools.partial(finish, h - 1))
    for step in range(total + lag):
        if step < total:
            relay(step)
            if step + AHEAD < total:
                send_own(step + AHEAD)
        if 1 <= step < total + 1:
            crossed(step - 1)
        if step >= lag:
            shared_in(step - lag)
        for task in tasks.pop(step, []):
            task()
    for step in sorted(tasks):
        for task in tasks[step]:
            task()
    finish(nh - 1)

    for copy in started:
        copy.wait_send()
    for h in range(nh):
        outputs[h].wait()
        cols = pl.ds(pl.multiple_of(((1 - core) * nh + h) * head_dim, LANES), head_dim)
        await_at(out_ref.at[:, cols], give_recv.at[h])


def per_device(inputs, query_weight, key_weight, value_weight, lambda_weight, log_decay, norm_gain):
    count = lax.axis_size("ctx")
    chips = count // 2
    bits = count.bit_length() - 1
    length, width = inputs.shape[1:]
    depth, wide = value_weight.shape
    heads = log_decay.shape[2]
    levels = lambda_weight.shape[1] // heads
    state_dim = query_weight.shape[1]
    head_dim = wide // heads
    nh = heads // 2
    lams = lambda_weight.shape[1] // 2
    total = 3 + nh * PIECES
    f32, bf16 = jnp.float32, jnp.bfloat16
    vmem = pl.BlockSpec(memory_space=pltpu.VMEM)
    anywhere = pl.BlockSpec(memory_space=pl.ANY)
    dma = pltpu.SemaphoreType.DMA
    out = pl.pallas_call(
        functools.partial(fused_kernel, levels),
        out_shape=jax.ShapeDtypeStruct((length, wide), bf16),
        in_specs=[anywhere] * 6 + [vmem],
        out_specs=anywhere,
        scratch_shapes=[
            pltpu.VMEM((2 * length, width), bf16),
            pltpu.VMEM((2 * nh, length), f32),
            pltpu.VMEM((4, depth, state_dim), bf16),
            pltpu.VMEM((4, depth, state_dim), bf16),
            pltpu.VMEM((4, lams, depth), bf16),
            pltpu.VMEM((nh, 4, depth, head_dim), bf16),
            pltpu.VMEM((2 * length, 2 * state_dim), bf16),
            pltpu.VMEM((2 * length, lams), f32),
            pltpu.VMEM((nh, 2 * length, head_dim), bf16),
            pltpu.VMEM((2, length, length), f32),
            pltpu.VMEM((2 * nh, length), f32),
            pltpu.VMEM((length, 2 * nh), f32),
            pltpu.VMEM((length, 2 * nh), f32),
            pltpu.VMEM((length, 2 * nh), f32),
            pltpu.VMEM((length, 2 * nh), f32),
            pltpu.VMEM((chips, nh, LANES), f32),
            pltpu.VMEM((bits, 3, nh, LANES), f32),
            pltpu.VMEM((nh, state_dim, head_dim), f32),
            pltpu.VMEM((bits, nh, state_dim, head_dim), bf16),
            pltpu.VMEM((bits, nh, state_dim, head_dim), bf16),
            pltpu.VMEM((nh, 2 * length, head_dim), f32),
            pltpu.VMEM((nh, 2 * length, head_dim), bf16),
            dma((5 + nh,)),
            dma((2,)),
            dma((2,)),
            dma((2, total)),
            dma((2, total)),
            dma((2, total)),
            dma((2, total)),
            dma((3, total)),
            dma((3, total)),
            dma((2,)),
            dma((2,)),
            dma((chips,)),
            dma((chips,)),
            dma((bits, nh)),
            dma((bits, nh)),
            dma((nh,)),
            dma((nh,)),
            dma((nh,)),
        ],
        compiler_params=pltpu.CompilerParams(
            collective_id=0, has_side_effects=True, vmem_limit_bytes=VMEM_LIMIT),
        name="gather_mix",
    )(inputs[0], query_weight, key_weight, lambda_weight.T, value_weight, log_decay[0].T,
      norm_gain[None])
    return out[None]


def solution(mesh):
    return jax.shard_map(
        per_device,
        mesh=mesh,
        in_specs=(
            P("dp", "ctx", None),
            P("dp", None),
            P("dp", None),
            P("dp", None),
            P("dp", None),
            P("dp", "ctx", None),
            P(),
        ),
        out_specs=P("dp", "ctx", None),
        check_vma=False,
    )
```

```python
import functools
import math

import jax
import jax.numpy as jnp
from jax import lax
from jax.experimental import pallas as pl
from jax.experimental.pallas import tpu as pltpu
from jax.sharding import PartitionSpec as P

HIGHEST = lax.Precision.HIGHEST
MESH = pl.DeviceIdType.MESH
VMEM_LIMIT = 60 * 1024 * 1024

AHEAD = 2
SHARE = 5 / 16
LATE = (0.0, 0.0)
LANES = 128


def flipped(index, mask):
    out = index
    for power in range(mask.bit_length()):
        if mask >> power & 1:
            step = 1 << power
            out = out + step - 2 * step * ((index // step) % 2)
    return out


def fused_kernel(levels, x_ref, q_ref, k_ref, lam_t_ref, v_ref, decay_ref, gain_ref, out_ref,
                 xs, dec, big_q, big_k, big_l, big_v, qk, lam, val, score, cum_rows, cum_cols,
                 grow, reach_grow, remain, logs, coef, state, sent, got, mixed, result,
                 load_sem, swap_send, swap_recv, own_send, own_recv, relay_send, relay_recv,
                 z_send, z_recv, core_send, core_recv, log_send, log_recv, st_send, st_recv,
                 out_sem, give_send, give_recv):
    f32, bf16 = jnp.float32, jnp.bfloat16
    count = lax.axis_size("ctx")
    chips = count // 2
    bits = count.bit_length() - 1
    dp = lax.axis_index("dp")
    ctx = lax.axis_index("ctx")
    x_at, y_at = dp % 2, dp // 2
    core = ctx % 2
    side = (ctx // 2) % 2
    length = x_ref.shape[0]
    depth, wide = v_ref.shape
    nh = decay_ref.shape[0] // 2
    lams = lam_t_ref.shape[0] // 2
    head_dim = wide // (2 * nh)
    state_dim = q_ref.shape[1]
    inner = length.bit_length()
    scale = 1.0 / math.sqrt(state_dim)
    to_x = {"dp": y_at * 2 + (1 - x_at)}
    to_y = {"dp": (1 - y_at) * 2 + x_at}
    to_core = {"ctx": flipped(ctx, 1)}
    to_z = {"ctx": flipped(ctx, 2)}
    peers = [None] + [{"ctx": flipped(ctx, 2 * r)} for r in range(1, chips)]
    owners = (y_at * 2 + (1 - x_at), (1 - y_at) * 2 + x_at, (1 - y_at) * 2 + (1 - x_at), dp)
    started = []

    def remote(src, dst, out_sem_, in_sem, target):
        copy = pltpu.make_async_remote_copy(
            src_ref=src, dst_ref=dst, send_sem=out_sem_, recv_sem=in_sem,
            device_id=target, device_id_type=MESH)
        copy.start()
        started.append(copy)

    def await_at(spot, sem):
        pltpu.make_async_copy(spot, spot, sem).wait()

    barrier = pltpu.get_barrier_semaphore()
    greeted = [to_x, to_y, to_core] + peers[1:]
    for target in greeted:
        pl.semaphore_signal(barrier, inc=1, device_id=target, device_id_type=MESH)

    my_rows = pl.ds(pl.multiple_of(core * length, length), length)
    my_heads = pl.ds(pl.multiple_of(core * nh, nh), nh)
    their_heads = pl.ds(pl.multiple_of((1 - core) * nh, nh), nh)
    my_lams = pl.ds(pl.multiple_of(core * lams, 16), lams)
    my_cols = pl.ds(pl.multiple_of(core * nh * head_dim, LANES), nh * head_dim)

    def head_cols(h):
        return pl.ds(pl.multiple_of((core * nh + h) * head_dim, LANES), head_dim)

    local = [
        pltpu.make_async_copy(decay_ref.at[my_heads], dec.at[my_heads], load_sem.at[0]),
        pltpu.make_async_copy(x_ref, xs.at[my_rows], load_sem.at[1]),
        pltpu.make_async_copy(q_ref, big_q.at[3], load_sem.at[2]),
        pltpu.make_async_copy(k_ref, big_k.at[3], load_sem.at[3]),
        pltpu.make_async_copy(lam_t_ref.at[my_lams], big_l.at[3], load_sem.at[4]),
    ] + [pltpu.make_async_copy(v_ref.at[:, head_cols(h)], big_v.at[h, 3], load_sem.at[5 + h])
         for h in range(nh)]

    half = depth // 2
    cut = min(lams, LANES)
    lam_parts = [(0, cut)] + ([(cut, lams)] if cut < lams else [])
    pieces = [(k_ref, None, big_k, core * half, core * half, half),
              (q_ref, None, big_q, core * half, core * half, half),
              (lam_t_ref, None, big_l, core * lams, 0, cut)]
    pieces += [(v_ref, head_cols(h), big_v.at[h], 0, 0, depth) for h in range(nh)]
    pieces += [(lam_t_ref, None, big_l, core * lams + low, low, high - low)
               for low, high in lam_parts[1:]]
    total = len(pieces)
    share = [SHARE] * total
    share[total - len(LATE):] = LATE

    def shares(i):
        n = pieces[i][5]
        shared = int(n * share[i] / 16 + 0.5) * 16
        direct = n - shared
        first = (direct // 2 + 15) // 16 * 16
        return shared, direct, first

    def rows_at(base, start, size):
        return pl.ds(pl.multiple_of(base + start, 16), size)

    def send_own(i):
        src, cols, buf, src_base, base, n = pieces[i]
        shared, direct, first = shares(i)
        rows = rows_at(src_base, side * shared, direct)
        from_ = src.at[rows] if cols is None else src.at[rows, cols]
        for way, target in enumerate((to_x, to_y)):
            remote(from_, buf.at[way, rows_at(base, side * shared, direct)],
                   own_send.at[way, i], own_recv.at[way, i], target)

    def relay(i):
        src, cols, buf, src_base, base, n = pieces[i]
        shared, direct, first = shares(i)
        for way in range(2):
            await_at(buf.at[way, rows_at(base, side * shared, direct)], own_recv.at[way, i])
        for way, target, start, size in ((0, to_y, 0, first), (1, to_x, first, direct - first)):
            rows = rows_at(base, side * shared + start, size)
            remote(buf.at[way, rows], buf.at[2, rows], relay_send.at[way, i],
                   relay_recv.at[way, i], target)
        if shared > 0:
            for way in range(2):
                pass_on(i, way)

    def pass_on(i, way):
        src, cols, buf, src_base, base, n = pieces[i]
        shared, direct, first = shares(i)
        rows = rows_at(base, side * direct, shared)
        remote(buf.at[way, rows], buf.at[way, rows], z_send.at[way, i], z_recv.at[way, i], to_z)

    def crossed(i):
        src, cols, buf, src_base, base, n = pieces[i]
        shared, direct, first = shares(i)
        for way, start, size in ((0, 0, first), (1, first, direct - first)):
            await_at(buf.at[2, rows_at(base, side * shared + start, size)], relay_recv.at[way, i])
        if shared > 0:
            pass_on(i, 2)

    def shared_in(i):
        src, cols, buf, src_base, base, n = pieces[i]
        shared, direct, first = shares(i)
        if shared > 0:
            for way in range(3):
                await_at(
                    buf.at[way, rows_at(base, (1 - side) * direct, shared)], z_recv.at[way, i])
        if i < 2:
            rows = rows_at(base, 0, n)
            spot = buf.at[pl.ds(0, 3), rows]
            remote(spot, spot, core_send.at[i], core_recv.at[i], to_core)

    def own_part(way):
        return pl.ds(pl.multiple_of(owners[way] * depth, depth), depth)

    plain = (((1,), (0,)), ((), ()))
    turned = (((1,), (1,)), ((), ()))

    def gathered(weights, dims, ways=(3, 0, 1, 2), acc=None):
        for way in ways:
            term = lax.dot_general(
                xs[:, own_part(way)], weights(way), dims, preferred_element_type=f32)
            acc = term if acc is None else acc + term
        return acc

    def task_k():
        await_at(big_k.at[pl.ds(0, 3), rows_at((1 - core) * half, 0, half)], core_recv.at[0])
        qk[:, state_dim:] = gathered(lambda way: big_k[way], plain).astype(bf16)

    def task_q():
        await_at(big_q.at[pl.ds(0, 3), rows_at((1 - core) * half, 0, half)], core_recv.at[1])
        qk[:, :state_dim] = gathered(lambda way: big_q[way], plain).astype(bf16)
        row = lax.broadcasted_iota(jnp.int32, (length, length), 0)
        col = lax.broadcasted_iota(jnp.int32, (length, length), 1)
        for blk in range(2):
            rows = slice(blk * length, (blk + 1) * length)
            full = lax.dot_general(
                qk[rows, :state_dim], qk[rows, state_dim:], turned, preferred_element_type=f32)
            score[blk] = jnp.where(row >= col, full * scale, 0.0)

    def task_lam(part):
        low, high = lam_parts[part]
        lam[part, :, :high - low] = jax.nn.softplus(
            gathered(lambda way: big_l[way, low:high], turned))

    def lam_at(rows, at):
        part = 0 if at < cut else 1
        at -= part * cut
        return lam[part, rows, at:at + 1]

    def task_early(h):
        mixed[h] = gathered(lambda way: big_v[h, way], plain, (3,))

    def task_sums():
        row = lax.broadcasted_iota(jnp.int32, (length, length), 0)
        col = lax.broadcasted_iota(jnp.int32, (length, length), 1)
        below = (row >= col).astype(f32)
        decays = dec[...]
        ones = jnp.ones((length, LANES), f32)
        sums = jnp.dot(decays, ones, precision=HIGHEST, preferred_element_type=f32)
        logs[0] = sums[:nh] + sums[nh:]
        coef[0, 0] = jnp.exp(sums[nh:])
        for r in range(1, chips):
            remote(logs.at[0], logs.at[r], log_send.at[r], log_recv.at[r], peers[r])
        cum_col = lax.dot_general(
            below, decays, turned, precision=HIGHEST, preferred_element_type=f32)
        cum_rows[...] = lax.dot_general(
            decays, below, turned, precision=HIGHEST, preferred_element_type=f32)
        moved = jnp.concatenate((jnp.zeros((nh, length), f32), decays[:nh]), axis=0)
        before = lax.dot_general(
            jnp.ones((length, length), f32), moved, turned, precision=HIGHEST,
            preferred_element_type=f32)
        cum_cols[...] = cum_col
        grow[...] = jnp.exp(cum_col) * scale
        reach_grow[...] = jnp.exp(cum_col + before) * scale
        remain[...] = jnp.exp(cum_col[length - 1:length] - cum_col)

    def task_coef():
        for r in range(1, chips):
            await_at(logs.at[r], log_recv.at[r])
        own_log = logs[0]
        carry_log = jnp.zeros_like(own_log)
        for b in range(1, bits):
            upper = ((ctx // (1 << b)) % 2).astype(f32)
            step = 1 << (b - 1)
            other = logs[step]
            for r in range(step + 1, 2 * step):
                other = other + logs[r]
            coef[b, 0] = jnp.exp(carry_log) * upper
            coef[b, 1] = jnp.where(upper > 0, 1.0, jnp.exp(other))
            coef[b, 2] = jnp.where(upper > 0, jnp.exp(own_log), 1.0)
            carry_log = carry_log + upper * other
            own_log = own_log + other

    def upper_at(b):
        return (ctx // (1 << b)) % 2 == 1

    def merges_at(b):
        return ctx // (2 << b) != count // (2 << b) - 1

    def state_copy(h, b):
        return pltpu.make_async_remote_copy(
            src_ref=sent.at[b, h], dst_ref=got.at[b, h], send_sem=st_send.at[b, h],
            recv_sem=st_recv.at[b, h], device_id=peers[1 << (b - 1)], device_id_type=MESH)

    def sends_at(b):
        return jnp.logical_or(jnp.logical_not(upper_at(b)), merges_at(b))

    def takes_at(b):
        return jnp.logical_or(upper_at(b), merges_at(b))

    def send_state(h, b):
        @pl.when(sends_at(b))
        def _():
            state_copy(h, b).start()

    def await_state(h, b):
        @pl.when(takes_at(b))
        def _():
            await_at(got.at[b, h], st_recv.at[b, h])

    def task_head(h):
        val[h] = gathered(
            lambda way: big_v[h, way], plain, (0, 1, 2), mixed[h]).astype(bf16)
        blocks = []
        for blk in range(2):
            rows = slice(blk * length, (blk + 1) * length)
            at = blk * nh + h
            keyed = (qk[rows, state_dim:].astype(f32) * remain[:, at:at + 1]).astype(bf16)
            blocks.append(lax.dot_general(
                keyed, val[h, rows], (((0,), (0,)), ((), ())), preferred_element_type=f32))
        sent[0, h] = blocks[0].astype(bf16)
        if bits > 1:
            whole = coef[0, 0, h:h + 1] * blocks[0] + blocks[1]
            state[h] = whole
            sent[1, h] = whole.astype(bf16)
            send_state(h, 1)

    tile = 128
    tiles = length // tile

    def task_near(h, blk):
        trow = lax.broadcasted_iota(jnp.int32, (tile, tile), 0)
        tcol = lax.broadcasted_iota(jnp.int32, (tile, tile), 1)
        differ = jnp.bitwise_xor(trow, tcol)
        deep = tile.bit_length() - 1
        base = h * levels
        at_cum = blk * nh + h
        low = blk * length
        for ti in range(tiles):
            rows = slice(low + ti * tile, low + (ti + 1) * tile)
            here = slice(ti * tile, (ti + 1) * tile)
            acc = None
            for tj in range(ti + 1):
                cols = slice(tj * tile, (tj + 1) * tile)
                if ti == tj:
                    weight = jnp.broadcast_to(lam_at(rows, base), (tile, tile))
                    for level in range(1, deep + 1):
                        at = base + level
                        weight = jnp.where(
                            differ >= 1 << (level - 1), lam_at(rows, at), weight)
                else:
                    at = base + deep + (ti ^ tj).bit_length()
                    weight = lam_at(rows, at)
                distance = cum_cols[here, at_cum:at_cum + 1] - cum_rows[at_cum:at_cum + 1, cols]
                decay = jnp.exp(jnp.minimum(distance, 0.0))
                mix = (weight * (decay * score[blk, here, cols])).astype(bf16)
                term = jnp.dot(
                    mix, val[h, low + tj * tile:low + (tj + 1) * tile],
                    preferred_element_type=f32)
                acc = term if acc is None else acc + term
            if blk == 1:
                reach = jnp.dot(qk[rows, :state_dim], sent[0, h], preferred_element_type=f32)
                at = base + inner
                acc = acc + lam_at(rows, at) * grow[here, at_cum:at_cum + 1] * reach
            mixed[h, rows] = acc

    def far(h, b):
        carried = (coef[b, 0, h:h + 1] * got[b, h].astype(f32)).astype(bf16)
        reach = jnp.dot(qk[:, :state_dim], carried, preferred_element_type=f32)
        at = h * levels + inner + b
        grown = jnp.concatenate((reach_grow[:, h:h + 1], reach_grow[:, nh + h:nh + h + 1]), axis=0)
        return lam_at(slice(None), at) * grown * reach

    def task_merge(h, b):
        await_state(h, b)

        @pl.when(merges_at(b))
        def _():
            block = coef[b, 1, h:h + 1] * state[h] + coef[b, 2, h:h + 1] * got[b, h].astype(f32)
            state[h] = block
            sent[b + 1, h] = block.astype(bf16)
        send_state(h, b + 1)

    def task_far(h, b):
        @pl.when(upper_at(b))
        def _():
            mixed[h] += far(h, b)

    def task_finish(h):
        if bits > 1:
            await_state(h, bits - 1)
            task_far(h, bits - 1)
        whole = mixed[h]
        mean_square = jnp.mean(whole * whole, axis=-1, keepdims=True)
        gain = gain_ref[:, head_cols(h)]
        result[h] = (whole * lax.rsqrt(mean_square + 1e-05) * gain).astype(bf16)
        remote(result.at[h, pl.ds(pl.multiple_of((1 - core) * length, length), length)],
               out_ref.at[:, head_cols(h)], give_send.at[h], give_recv.at[h], to_core)
        copy = pltpu.make_async_copy(
            result.at[h, my_rows], out_ref.at[:, head_cols(h)], out_sem.at[h])
        copy.start()
        return copy

    for copy in local:
        copy.start()
    pl.semaphore_wait(barrier, len(greeted))
    for i in range(AHEAD):
        send_own(i)
    remote(decay_ref.at[their_heads], dec.at[my_heads], swap_send.at[0], swap_recv.at[0], to_core)
    remote(x_ref, xs.at[my_rows], swap_send.at[1], swap_recv.at[1], to_core)

    def task_loads():
        for copy in local[1:]:
            copy.wait()
        await_at(
            xs.at[pl.ds(pl.multiple_of((1 - core) * length, length), length)], swap_recv.at[1])

    def task_decays():
        local[0].wait()
        await_at(dec.at[their_heads], swap_recv.at[0])
        task_sums()

    outputs = []

    def task_output(h):
        outputs.append(task_finish(h))

    def call(task, *what):
        return functools.partial(task, *what)

    done = [i + (2 if shares(i)[0] > 0 else 1) for i in range(total)]
    last_lam = len(lam_parts) - 1
    tasks = {}

    ranks = {task_head: 1, task_lam: 2, task_merge: 3, task_output: 4, task_near: 5, task_far: 6}

    def plan(step, *what):
        tasks.setdefault(step, []).extend(what)
        tasks[step].sort(key=lambda task: ranks.get(task.func, 0))

    plan(0, call(task_decays), call(task_loads))
    for h in range(nh):
        plan(h % 3, call(task_early, h))
    plan(2, call(task_coef))
    plan(done[0] + 1, call(task_k))
    plan(done[1] + 1, call(task_q))
    plan(max(done[1] + 1, done[2]), call(task_lam, 0))
    mids = range(1, bits - 1)
    for h in range(nh):
        at = max(done[3 + h], done[1] + 1)
        last = h == nh - 1
        plan(at, call(task_head, h))
        after = at if last else at + 1
        if (h + 1) * levels > cut:
            after = max(after, done[total - 1])
        ready = max(at + 1, after - 1) if last else at + 1
        plan(ready, *[call(task_merge, h, b) for b in mids])
        if h * levels <= cut < (h + 1) * levels:
            plan(after, *[call(task_lam, p) for p in range(1, last_lam + 1)])
        plan(after, call(task_near, h, 0), call(task_near, h, 1))
        plan(max(ready, after), *[call(task_far, h, b) for b in mids])
        plan(max(ready, after) + 1, call(task_output, h))
    for step in range(total + 2):
        if step < total:
            relay(step)
            if step + AHEAD < total:
                send_own(step + AHEAD)
        if 1 <= step < total + 1:
            crossed(step - 1)
        for i in (step - 2, step - 1):
            if 0 <= i < total and done[i] == step:
                shared_in(i)
        for task in tasks.pop(step, []):
            task()
    for step in sorted(tasks):
        for task in tasks[step]:
            task()
    for b in range(1, bits):
        @pl.when(sends_at(b))
        def _(b=b):
            for h in range(nh):
                state_copy(h, b).wait_send()

    for copy in started:
        copy.wait_send()
    for h in range(nh):
        outputs[h].wait()
        cols = pl.ds(pl.multiple_of(((1 - core) * nh + h) * head_dim, LANES), head_dim)
        await_at(out_ref.at[:, cols], give_recv.at[h])


def per_device(inputs, query_weight, key_weight, value_weight, lambda_weight, log_decay, norm_gain):
    count = lax.axis_size("ctx")
    chips = count // 2
    bits = count.bit_length() - 1
    length, width = inputs.shape[1:]
    depth, wide = value_weight.shape
    heads = log_decay.shape[2]
    levels = lambda_weight.shape[1] // heads
    state_dim = query_weight.shape[1]
    head_dim = wide // heads
    nh = heads // 2
    lams = lambda_weight.shape[1] // 2
    total = 3 + nh + (1 if lams > LANES else 0)
    f32, bf16 = jnp.float32, jnp.bfloat16
    vmem = pl.BlockSpec(memory_space=pltpu.VMEM)
    anywhere = pl.BlockSpec(memory_space=pl.ANY)
    dma = pltpu.SemaphoreType.DMA
    out = pl.pallas_call(
        functools.partial(fused_kernel, levels),
        out_shape=jax.ShapeDtypeStruct((length, wide), bf16),
        in_specs=[anywhere] * 6 + [vmem],
        out_specs=anywhere,
        scratch_shapes=[
            pltpu.VMEM((2 * length, width), bf16),
            pltpu.VMEM((2 * nh, length), f32),
            pltpu.VMEM((4, depth, state_dim), bf16),
            pltpu.VMEM((4, depth, state_dim), bf16),
            pltpu.VMEM((4, lams, depth), bf16),
            pltpu.VMEM((nh, 4, depth, head_dim), bf16),
            pltpu.VMEM((2 * length, 2 * state_dim), bf16),
            pltpu.VMEM((2, 2 * length, LANES), f32),
            pltpu.VMEM((nh, 2 * length, head_dim), bf16),
            pltpu.VMEM((2, length, length), f32),
            pltpu.VMEM((2 * nh, length), f32),
            pltpu.VMEM((length, 2 * nh), f32),
            pltpu.VMEM((length, 2 * nh), f32),
            pltpu.VMEM((length, 2 * nh), f32),
            pltpu.VMEM((length, 2 * nh), f32),
            pltpu.VMEM((chips, nh, LANES), f32),
            pltpu.VMEM((bits, 3, nh, LANES), f32),
            pltpu.VMEM((nh, state_dim, head_dim), f32),
            pltpu.VMEM((bits, nh, state_dim, head_dim), bf16),
            pltpu.VMEM((bits, nh, state_dim, head_dim), bf16),
            pltpu.VMEM((nh, 2 * length, head_dim), f32),
            pltpu.VMEM((nh, 2 * length, head_dim), bf16),
            dma((5 + nh,)),
            dma((2,)),
            dma((2,)),
            dma((2, total)),
            dma((2, total)),
            dma((2, total)),
            dma((2, total)),
            dma((3, total)),
            dma((3, total)),
            dma((2,)),
            dma((2,)),
            dma((chips,)),
            dma((chips,)),
            dma((bits, nh)),
            dma((bits, nh)),
            dma((nh,)),
            dma((nh,)),
            dma((nh,)),
        ],
        compiler_params=pltpu.CompilerParams(
            collective_id=0, has_side_effects=True, vmem_limit_bytes=VMEM_LIMIT),
        name="gather_mix",
    )(inputs[0], query_weight, key_weight, lambda_weight.T, value_weight, log_decay[0].T,
      norm_gain[None])
    return out[None]


def solution(mesh):
    return jax.shard_map(
        per_device,
        mesh=mesh,
        in_specs=(
            P("dp", "ctx", None),
            P("dp", None),
            P("dp", None),
            P("dp", None),
            P("dp", None),
            P("dp", "ctx", None),
            P(),
        ),
        out_specs=P("dp", "ctx", None),
        check_vma=False,
    )
```

```python
import functools
import math

import jax
import jax.numpy as jnp
from jax import lax
from jax.experimental import pallas as pl
from jax.experimental.pallas import tpu as pltpu
from jax.sharding import PartitionSpec as P

HIGHEST = lax.Precision.HIGHEST
MESH = pl.DeviceIdType.MESH
VMEM_LIMIT = 60 * 1024 * 1024

AHEAD = 2.0
SHARE = 6.5 / 16
SHARE_FIRST = 8 / 16
SHARE_LATE = (7 / 16, 7 / 16, 8 / 16)
CUT = 128
LAST_PARTS = 2
LANES = 128


def flipped(index, mask):
    out = index
    for power in range(mask.bit_length()):
        if mask >> power & 1:
            step = 1 << power
            out = out + step - 2 * step * ((index // step) % 2)
    return out


def fused_kernel(levels, x_ref, q_ref, k_ref, lam_t_ref, v_ref, decay_ref, gain_ref, out_ref,
                 xs, dec, big_q, big_k, big_l, big_v, qk, lam, val, score, cum_rows, cum_cols,
                 grow, reach_grow, remain, keys_t, logs, coef, state, sent, got, mixed, result,
                 load_sem, swap_send, swap_recv, own_send, own_recv, relay_send, relay_recv,
                 z_send, z_recv, core_send, core_recv, log_send, log_recv, st_send, st_recv,
                 out_sem, give_send, give_recv,
                 greet_up, greet_down):
    f32, bf16 = jnp.float32, jnp.bfloat16
    count = lax.axis_size("ctx")
    chips = count // 2
    bits = count.bit_length() - 1
    dp = lax.axis_index("dp")
    ctx = lax.axis_index("ctx")
    x_at, y_at = dp % 2, dp // 2
    core = ctx % 2
    side = (ctx // 2) % 2
    length = x_ref.shape[0]
    depth, wide = v_ref.shape
    nh = decay_ref.shape[0] // 2
    lams = lam_t_ref.shape[0] // 2
    head_dim = wide // (2 * nh)
    state_dim = q_ref.shape[1]
    inner = length.bit_length()
    scale = 1.0 / math.sqrt(state_dim)
    to_x = {"dp": y_at * 2 + (1 - x_at)}
    to_y = {"dp": (1 - y_at) * 2 + x_at}
    to_core = {"ctx": flipped(ctx, 1)}
    to_z = {"ctx": flipped(ctx, 2)}
    peers = [None] + [{"ctx": flipped(ctx, 2 * r)} for r in range(1, chips)]
    owners = (y_at * 2 + (1 - x_at), (1 - y_at) * 2 + x_at, (1 - y_at) * 2 + (1 - x_at), dp)
    started = []

    def remote(src, dst, out_sem_, in_sem, target):
        copy = pltpu.make_async_remote_copy(
            src_ref=src, dst_ref=dst, send_sem=out_sem_, recv_sem=in_sem,
            device_id=target, device_id_type=MESH)
        copy.start()
        started.append(copy)

    def await_at(spot, sem):
        pltpu.make_async_copy(spot, spot, sem).wait()

    chip = ctx // 2
    below, above = chip > 0, chip < chips - 1
    to_below, to_above = {"ctx": (ctx + count - 2) % count}, {"ctx": (ctx + 2) % count}
    barrier = pltpu.get_barrier_semaphore()
    for target in (to_x, to_y, to_core):
        pl.semaphore_signal(barrier, inc=1, device_id=target, device_id_type=MESH)
    for there, target in ((below, to_below), (above, to_above)):
        @pl.when(there)
        def _(target=target):
            pl.semaphore_signal(barrier, inc=1, device_id=target, device_id_type=MESH)

    def greet_all():
        def pass_along(sem, first, then, target):
            @pl.when(first)
            def _():
                pl.semaphore_wait(sem, 1)

            @pl.when(then)
            def _():
                pl.semaphore_signal(sem, inc=1, device_id=target, device_id_type=MESH)

        @pl.when(chip >= chips // 2)
        def _():
            pass_along(greet_down, above, below, to_below)
        pass_along(greet_up, below, above, to_above)

        @pl.when(chip < chips // 2)
        def _():
            pass_along(greet_down, above, below, to_below)

    my_rows = pl.ds(pl.multiple_of(core * length, length), length)
    my_heads = pl.ds(pl.multiple_of(core * nh, nh), nh)
    their_heads = pl.ds(pl.multiple_of((1 - core) * nh, nh), nh)
    my_lams = pl.ds(pl.multiple_of(core * lams, 16), lams)
    my_cols = pl.ds(pl.multiple_of(core * nh * head_dim, LANES), nh * head_dim)

    def head_cols(h):
        return pl.ds(pl.multiple_of((core * nh + h) * head_dim, LANES), head_dim)

    local = [
        pltpu.make_async_copy(decay_ref.at[my_heads], dec.at[my_heads], load_sem.at[0]),
        pltpu.make_async_copy(x_ref, xs.at[my_rows], load_sem.at[1]),
        pltpu.make_async_copy(q_ref, big_q.at[3], load_sem.at[2]),
        pltpu.make_async_copy(k_ref, big_k.at[3], load_sem.at[3]),
        pltpu.make_async_copy(lam_t_ref.at[my_lams], big_l.at[3], load_sem.at[4]),
    ] + [pltpu.make_async_copy(v_ref.at[:, head_cols(h)], big_v.at[h, 3], load_sem.at[5 + h])
         for h in range(nh)]

    half = depth // 2
    cut = min(lams, CUT)
    lam_parts = [(0, cut)] + ([(cut, lams)] if cut < lams else [])
    pieces = [(k_ref, None, big_k, core * half, core * half, half),
              (q_ref, None, big_q, core * half, core * half, half),
              (lam_t_ref, None, big_l, core * lams, 0, cut)]
    parts = []
    for h in range(nh):
        size = depth // (LAST_PARTS if h == nh - 1 else 1)
        parts.append(range(len(pieces), len(pieces) + depth // size))
        pieces += [(v_ref, head_cols(h), big_v.at[h], low, low, size)
                   for low in range(0, depth, size)]
    pieces += [(lam_t_ref, None, big_l, core * lams + low, low, high - low)
               for low, high in lam_parts[1:]]
    total = len(pieces)
    weight = [piece[5] * (depth if piece[0] is lam_t_ref else head_dim) / (depth * head_dim)
              for piece in pieces]
    issued = []

    def send_ahead(step):
        while (len(issued) < total
               and sum(weight[step + 1:len(issued) + 1]) <= AHEAD):
            send_own(len(issued))
            issued.append(step)

    share = [SHARE_FIRST] * 3 + [SHARE] * (total - 3)
    share[total - len(SHARE_LATE):] = SHARE_LATE

    def shares(i):
        n = pieces[i][5]
        first = (n // 2 + 15) // 16 * 16
        shared = min(int(n * share[i] / 16 + 0.5) * 16, n - first)
        return shared, n - shared, first

    def rows_at(base, start, size):
        return pl.ds(pl.multiple_of(base + start, 16), size)

    def direct_start(way, shared):
        return (1 - side if way else side) * shared

    def send_own(i):
        src, cols, buf, src_base, base, n = pieces[i]
        shared, direct, first = shares(i)
        for way, target in enumerate((to_x, to_y)):
            start = direct_start(way, shared)
            rows = rows_at(src_base, start, direct)
            remote(src.at[rows] if cols is None else src.at[rows, cols],
                   buf.at[way, rows_at(base, start, direct)],
                   own_send.at[way, i], own_recv.at[way, i], target)

    def relays(i):
        src, cols, buf, src_base, base, n = pieces[i]
        shared, direct, first = shares(i)
        return ((0, to_y, rows_at(base, side * (n - first), first)),
                (1, to_x, rows_at(base, (1 - side) * first, n - first)))

    def relay(i):
        src, cols, buf, src_base, base, n = pieces[i]
        shared, direct, first = shares(i)
        for way in range(2):
            spot = buf.at[way, rows_at(base, direct_start(way, shared), direct)]
            await_at(spot, own_recv.at[way, i])
        for way, target, rows in relays(i):
            remote(buf.at[way, rows], buf.at[2, rows], relay_send.at[way, i],
                   relay_recv.at[way, i], target)
        if shared > 0:
            for way in range(2):
                rows = rows_at(base, (1 - side if way else side) * direct, shared)
                remote(buf.at[way, rows], buf.at[way, rows], z_send.at[way, i],
                       z_recv.at[way, i], to_z)

    def crossed(i):
        src, cols, buf, src_base, base, n = pieces[i]
        shared, direct, first = shares(i)
        for way, target, rows in relays(i):
            await_at(buf.at[2, rows], relay_recv.at[way, i])
        if shared > 0:
            for way in range(2):
                rows = rows_at(base, (side if way else 1 - side) * direct, shared)
                await_at(buf.at[way, rows], z_recv.at[way, i])
        if i < 2:
            spot = buf.at[pl.ds(0, 3), rows_at(base, 0, n)]
            remote(spot, spot, core_send.at[i], core_recv.at[i], to_core)

    def own_part(way, low=0, size=depth):
        return pl.ds(pl.multiple_of(owners[way] * depth + low, LANES), size)

    plain = (((1,), (0,)), ((), ()))
    turned = (((1,), (1,)), ((), ()))

    def gathered(weights, dims, ways=(3, 0, 1, 2), acc=None):
        for way in ways:
            term = lax.dot_general(
                xs[:, own_part(way)], weights(way), dims, preferred_element_type=f32)
            acc = term if acc is None else acc + term
        return acc

    def task_k():
        await_at(big_k.at[pl.ds(0, 3), rows_at((1 - core) * half, 0, half)], core_recv.at[0])
        keys = gathered(lambda way: big_k[way], plain).astype(bf16)
        qk[:, state_dim:] = keys
        keys_t[...] = keys.astype(f32).T

    def task_q():
        await_at(big_q.at[pl.ds(0, 3), rows_at((1 - core) * half, 0, half)], core_recv.at[1])
        qk[:, :state_dim] = gathered(lambda way: big_q[way], plain).astype(bf16)
        row = lax.broadcasted_iota(jnp.int32, (length, length), 0)
        col = lax.broadcasted_iota(jnp.int32, (length, length), 1)
        for blk in range(2):
            rows = slice(blk * length, (blk + 1) * length)
            full = lax.dot_general(
                qk[rows, :state_dim], qk[rows, state_dim:], turned, preferred_element_type=f32)
            score[blk] = jnp.where(row >= col, full * scale, 0.0)

    def task_lam(part):
        low, high = lam_parts[part]
        lam[part, :, :high - low] = jax.nn.softplus(
            gathered(lambda way: big_l[way, low:high], turned))

    def lam_at(rows, at):
        part = 0 if at < cut else 1
        at -= part * cut
        return lam[part, rows, at:at + 1]

    def task_early(h):
        mixed[h] = gathered(lambda way: big_v[h, way], plain, (3,))

    def task_sums():
        row = lax.broadcasted_iota(jnp.int32, (length, length), 0)
        col = lax.broadcasted_iota(jnp.int32, (length, length), 1)
        below = (row >= col).astype(f32)
        decays = dec[...]
        ones = jnp.ones((length, LANES), f32)
        sums = jnp.dot(decays, ones, precision=HIGHEST, preferred_element_type=f32)
        logs[0] = sums[:nh] + sums[nh:]
        coef[0, 0] = jnp.exp(sums[nh:])
        for r in range(1, chips):
            remote(logs.at[0], logs.at[r], log_send.at[r], log_recv.at[r], peers[r])
        cum_col = lax.dot_general(
            below, decays, turned, precision=HIGHEST, preferred_element_type=f32)
        cum_row = lax.dot_general(
            decays, below, turned, precision=HIGHEST, preferred_element_type=f32)
        cum_rows[...] = cum_row
        moved = jnp.concatenate((jnp.zeros((nh, length), f32), decays[:nh]), axis=0)
        before = lax.dot_general(
            jnp.ones((length, length), f32), moved, turned, precision=HIGHEST,
            preferred_element_type=f32)
        cum_cols[...] = cum_col
        grow[...] = jnp.exp(cum_col) * scale
        reach_grow[...] = jnp.exp(cum_col + before) * scale
        remain[...] = jnp.exp(cum_row[:, length - 1:length] - cum_row)

    def task_coef():
        for r in range(1, chips):
            await_at(logs.at[r], log_recv.at[r])
        own_log = logs[0]
        carry_log = jnp.zeros_like(own_log)
        for b in range(1, bits):
            upper = ((ctx // (1 << b)) % 2).astype(f32)
            step = 1 << (b - 1)
            other = logs[step]
            for r in range(step + 1, 2 * step):
                other = other + logs[r]
            coef[b, 0] = jnp.exp(carry_log) * upper
            coef[b, 1] = jnp.where(upper > 0, 1.0, jnp.exp(other))
            coef[b, 2] = jnp.where(upper > 0, jnp.exp(own_log), 1.0)
            carry_log = carry_log + upper * other
            own_log = own_log + other

    def upper_at(b):
        return (ctx // (1 << b)) % 2 == 1

    def merges_at(b):
        return ctx // (2 << b) != count // (2 << b) - 1

    def state_copy(h, b):
        return pltpu.make_async_remote_copy(
            src_ref=sent.at[b, h], dst_ref=got.at[b, h], send_sem=st_send.at[b, h],
            recv_sem=st_recv.at[b, h], device_id=peers[1 << (b - 1)], device_id_type=MESH)

    def sends_at(b):
        return jnp.logical_or(jnp.logical_not(upper_at(b)), merges_at(b))

    def takes_at(b):
        return jnp.logical_or(upper_at(b), merges_at(b))

    def send_state(h, b):
        @pl.when(sends_at(b))
        def _():
            state_copy(h, b).start()

    def await_state(h, b):
        @pl.when(takes_at(b))
        def _():
            await_at(got.at[b, h], st_recv.at[b, h])

    def add_part(h, p):
        low, size = pieces[parts[h][p]][4:]
        acc = mixed[h]
        for way in range(3):
            acc = acc + jnp.dot(
                xs[:, own_part(way, low, size)], big_v[h, way, low:low + size],
                preferred_element_type=f32)
        return acc

    def task_part(h, p):
        mixed[h] = add_part(h, p)

    def task_head(h):
        val[h] = add_part(h, len(parts[h]) - 1).astype(bf16)
        blocks = []
        for blk in range(2):
            rows = slice(blk * length, (blk + 1) * length)
            at = blk * nh + h
            keyed = (keys_t[:, rows] * remain[at:at + 1]).astype(bf16)
            blocks.append(jnp.dot(keyed, val[h, rows], preferred_element_type=f32))
        sent[0, h] = blocks[0].astype(bf16)
        if bits > 1:
            whole = coef[0, 0, h:h + 1] * blocks[0] + blocks[1]
            state[h] = whole
            sent[1, h] = whole.astype(bf16)
            send_state(h, 1)

    tile = 128
    tiles = length // tile

    def task_near(h, blk):
        trow = lax.broadcasted_iota(jnp.int32, (tile, tile), 0)
        tcol = lax.broadcasted_iota(jnp.int32, (tile, tile), 1)
        differ = jnp.bitwise_xor(trow, tcol)
        deep = tile.bit_length() - 1
        base = h * levels
        at_cum = blk * nh + h
        low = blk * length
        for ti in range(tiles):
            rows = slice(low + ti * tile, low + (ti + 1) * tile)
            here = slice(ti * tile, (ti + 1) * tile)
            acc = None
            for tj in range(ti + 1):
                cols = slice(tj * tile, (tj + 1) * tile)
                if ti == tj:
                    weight = jnp.broadcast_to(lam_at(rows, base), (tile, tile))
                    for level in range(1, deep + 1):
                        at = base + level
                        weight = jnp.where(
                            differ >= 1 << (level - 1), lam_at(rows, at), weight)
                else:
                    at = base + deep + (ti ^ tj).bit_length()
                    weight = lam_at(rows, at)
                distance = cum_cols[here, at_cum:at_cum + 1] - cum_rows[at_cum:at_cum + 1, cols]
                decay = jnp.exp(jnp.minimum(distance, 0.0))
                mix = (weight * (decay * score[blk, here, cols])).astype(bf16)
                term = jnp.dot(
                    mix, val[h, low + tj * tile:low + (tj + 1) * tile],
                    preferred_element_type=f32)
                acc = term if acc is None else acc + term
            if blk == 1:
                reach = jnp.dot(qk[rows, :state_dim], sent[0, h], preferred_element_type=f32)
                at = base + inner
                acc = acc + lam_at(rows, at) * grow[here, at_cum:at_cum + 1] * reach
            mixed[h, rows] = acc

    def far(h, b):
        carried = (coef[b, 0, h:h + 1] * got[b, h].astype(f32)).astype(bf16)
        reach = jnp.dot(qk[:, :state_dim], carried, preferred_element_type=f32)
        at = h * levels + inner + b
        grown = jnp.concatenate((reach_grow[:, h:h + 1], reach_grow[:, nh + h:nh + h + 1]), axis=0)
        return lam_at(slice(None), at) * grown * reach

    def task_merge(h, b):
        await_state(h, b)

        @pl.when(merges_at(b))
        def _():
            block = coef[b, 1, h:h + 1] * state[h] + coef[b, 2, h:h + 1] * got[b, h].astype(f32)
            state[h] = block
            sent[b + 1, h] = block.astype(bf16)
        send_state(h, b + 1)

    def task_far(h, b):
        @pl.when(upper_at(b))
        def _():
            mixed[h] += far(h, b)

    def task_finish(h):
        if bits > 1:
            await_state(h, bits - 1)
            task_far(h, bits - 1)
        whole = mixed[h]
        mean_square = jnp.mean(whole * whole, axis=-1, keepdims=True)
        gain = gain_ref[:, head_cols(h)]
        result[h] = (whole * lax.rsqrt(mean_square + 1e-05) * gain).astype(bf16)
        remote(result.at[h, pl.ds(pl.multiple_of((1 - core) * length, length), length)],
               out_ref.at[:, head_cols(h)], give_send.at[h], give_recv.at[h], to_core)
        copy = pltpu.make_async_copy(
            result.at[h, my_rows], out_ref.at[:, head_cols(h)], out_sem.at[h])
        copy.start()
        return copy

    for copy in local:
        copy.start()
    pl.semaphore_wait(barrier, 3 + below.astype(jnp.int32) + above.astype(jnp.int32))
    send_ahead(-1)
    remote(decay_ref.at[their_heads], dec.at[my_heads], swap_send.at[0], swap_recv.at[0], to_core)
    remote(x_ref, xs.at[my_rows], swap_send.at[1], swap_recv.at[1], to_core)
    greet_all()

    def task_loads():
        for copy in local[1:]:
            copy.wait()
        await_at(
            xs.at[pl.ds(pl.multiple_of((1 - core) * length, length), length)], swap_recv.at[1])

    def task_decays():
        local[0].wait()
        await_at(dec.at[their_heads], swap_recv.at[0])
        task_sums()

    outputs = []

    def task_output(h):
        outputs.append(task_finish(h))

    def call(task, *what):
        return functools.partial(task, *what)

    tasks = {}
    final = total

    def plan(step, rank, task, *what):
        tasks.setdefault(min(step, final), []).append((rank, call(task, *what)))

    plan(0, 0, task_decays)
    plan(0, 0, task_loads)
    for h in range(nh):
        plan(h // 3, 0, task_early, h)
    plan(2, 0, task_coef)
    plan(2, 1, task_k)
    plan(3, 0, task_q)
    plan(3, 1, task_lam, 0)
    for p in range(1, len(lam_parts)):
        plan(final, 2, task_lam, p)
    for h in range(nh):
        at = parts[h][-1] + 1
        for p in range(len(parts[h]) - 1):
            plan(parts[h][p] + 1, 0, task_part, h, p)
        plan(at, 1, task_head, h)
        late = (h + 1) * levels > cut
        after = final if late else at + 1
        for b in range(1, bits - 1):
            plan(at + 1, 3, task_merge, h, b)
            plan(max(after, at + 1), 6, task_far, h, b)
        for blk in range(2):
            plan(after, 5, task_near, h, blk)
        out_step = max(after, at + 1) + 1
        plan(out_step, 4 if out_step <= final else 7, task_output, h)
    for step in range(total + 1):
        if step < total:
            relay(step)
            send_ahead(step)
        if step >= 1:
            crossed(step - 1)
        for rank, task in sorted(tasks.pop(step, []), key=lambda entry: entry[0]):
            task()
    for b in range(1, bits):
        @pl.when(sends_at(b))
        def _(b=b):
            for h in range(nh):
                state_copy(h, b).wait_send()

    for copy in started:
        copy.wait_send()
    for h in range(nh):
        outputs[h].wait()
        cols = pl.ds(pl.multiple_of(((1 - core) * nh + h) * head_dim, LANES), head_dim)
        await_at(out_ref.at[:, cols], give_recv.at[h])


def per_device(inputs, query_weight, key_weight, value_weight, lambda_weight, log_decay, norm_gain):
    count = lax.axis_size("ctx")
    chips = count // 2
    bits = count.bit_length() - 1
    length, width = inputs.shape[1:]
    depth, wide = value_weight.shape
    heads = log_decay.shape[2]
    levels = lambda_weight.shape[1] // heads
    state_dim = query_weight.shape[1]
    head_dim = wide // heads
    nh = heads // 2
    lams = lambda_weight.shape[1] // 2
    total = 3 + nh - 1 + LAST_PARTS + (1 if lams > CUT else 0)
    f32, bf16 = jnp.float32, jnp.bfloat16
    vmem = pl.BlockSpec(memory_space=pltpu.VMEM)
    anywhere = pl.BlockSpec(memory_space=pl.ANY)
    dma = pltpu.SemaphoreType.DMA
    out = pl.pallas_call(
        functools.partial(fused_kernel, levels),
        out_shape=pltpu.VMEM((length, wide), bf16),
        in_specs=[anywhere] * 6 + [vmem],
        out_specs=anywhere,
        scratch_shapes=[
            pltpu.VMEM((2 * length, width), bf16),
            pltpu.VMEM((2 * nh, length), f32),
            pltpu.VMEM((4, depth, state_dim), bf16),
            pltpu.VMEM((4, depth, state_dim), bf16),
            pltpu.VMEM((4, lams, depth), bf16),
            pltpu.VMEM((nh, 4, depth, head_dim), bf16),
            pltpu.VMEM((2 * length, 2 * state_dim), bf16),
            pltpu.VMEM((2, 2 * length, LANES), f32),
            pltpu.VMEM((nh, 2 * length, head_dim), bf16),
            pltpu.VMEM((2, length, length), f32),
            pltpu.VMEM((2 * nh, length), f32),
            pltpu.VMEM((length, 2 * nh), f32),
            pltpu.VMEM((length, 2 * nh), f32),
            pltpu.VMEM((length, 2 * nh), f32),
            pltpu.VMEM((2 * nh, length), f32),
            pltpu.VMEM((state_dim, 2 * length), f32),
            pltpu.VMEM((chips, nh, LANES), f32),
            pltpu.VMEM((bits, 3, nh, LANES), f32),
            pltpu.VMEM((nh, state_dim, head_dim), f32),
            pltpu.VMEM((bits, nh, state_dim, head_dim), bf16),
            pltpu.VMEM((bits, nh, state_dim, head_dim), bf16),
            pltpu.VMEM((nh, 2 * length, head_dim), f32),
            pltpu.VMEM((nh, 2 * length, head_dim), bf16),
            dma((5 + nh,)),
            dma((2,)),
            dma((2,)),
            dma((2, total)),
            dma((2, total)),
            dma((2, total)),
            dma((2, total)),
            dma((2, total)),
            dma((2, total)),
            dma((2,)),
            dma((2,)),
            dma((chips,)),
            dma((chips,)),
            dma((bits, nh)),
            dma((bits, nh)),
            dma((nh,)),
            dma((nh,)),
            dma((nh,)),
            pltpu.SemaphoreType.REGULAR,
            pltpu.SemaphoreType.REGULAR,
        ],
        compiler_params=pltpu.CompilerParams(
            collective_id=0, has_side_effects=True, vmem_limit_bytes=VMEM_LIMIT),
        name="gather_mix",
    )(inputs[0], query_weight, key_weight, lambda_weight.T, value_weight, log_decay[0].T,
      norm_gain[None])
    return out[None]


def solution(mesh):
    return jax.shard_map(
        per_device,
        mesh=mesh,
        in_specs=(
            P("dp", "ctx", None),
            P("dp", None),
            P("dp", None),
            P("dp", None),
            P("dp", None),
            P("dp", "ctx", None),
            P(),
        ),
        out_specs=P("dp", "ctx", None),
        check_vma=False,
    )
```

```python
import functools
import math

import jax
import jax.numpy as jnp
from jax import lax
from jax.experimental import pallas as pl
from jax.experimental.pallas import tpu as pltpu
from jax.sharding import PartitionSpec as P

HIGHEST = lax.Precision.HIGHEST
MESH = pl.DeviceIdType.MESH
VMEM_LIMIT = 60 * 1024 * 1024

AHEAD = 2.0
SHARE = 6.5 / 16
SHARE_FIRST = 8 / 16
SHARE_LATE = (8/16,)*3
CUT = 128
LAST_PARTS = 2
DIRECT = 1
LANES = 128


def flipped(index, mask):
    out = index
    for power in range(mask.bit_length()):
        if mask >> power & 1:
            step = 1 << power
            out = out + step - 2 * step * ((index // step) % 2)
    return out


def fused_kernel(levels, x_ref, q_ref, k_ref, lam_t_ref, v_ref, decay_ref, gain_hbm, out_ref,
                 gain_ref, xs, dec, big_q, big_k, big_l, big_v, qk, lam, val, score, cum_rows, cum_cols,
                 grow, reach_grow, remain, keys_t, logs, coef, state, sent, got, got_far, mixed, result,
                 load_sem, swap_send, swap_recv, own_recv, cross_recv, piece_send, core_send,
                 core_recv, log_send, log_recv, st_send, st_recv, direct_send, out_sem,
                 give_send, give_recv, greet_up, greet_down):
    f32, bf16 = jnp.float32, jnp.bfloat16
    count = lax.axis_size("ctx")
    chips = count // 2
    bits = count.bit_length() - 1
    dp = lax.axis_index("dp")
    ctx = lax.axis_index("ctx")
    x_at, y_at = dp % 2, dp // 2
    core = ctx % 2
    side = (ctx // 2) % 2
    length = x_ref.shape[0]
    depth, wide = v_ref.shape
    nh = decay_ref.shape[0] // 2
    lams = lam_t_ref.shape[0] // 2
    head_dim = wide // (2 * nh)
    state_dim = q_ref.shape[1]
    inner = length.bit_length()
    scale = 1.0 / math.sqrt(state_dim)
    to_x = {"dp": y_at * 2 + (1 - x_at)}
    to_y = {"dp": (1 - y_at) * 2 + x_at}
    to_core = {"ctx": flipped(ctx, 1)}
    to_z = {"ctx": flipped(ctx, 2)}
    peers = [None] + [{"ctx": flipped(ctx, 2 * r)} for r in range(1, chips)]
    owners = (y_at * 2 + (1 - x_at), (1 - y_at) * 2 + x_at, (1 - y_at) * 2 + (1 - x_at), dp)
    def remote(src, dst, out_sem_, in_sem, target):
        pltpu.make_async_remote_copy(
            src_ref=src, dst_ref=dst, send_sem=out_sem_, recv_sem=in_sem,
            device_id=target, device_id_type=MESH).start()

    def await_at(spot, sem):
        pltpu.make_async_copy(spot, spot, sem).wait()

    chip = ctx // 2
    below, above = chip > 0, chip < chips - 1
    to_below, to_above = {"ctx": (ctx + count - 2) % count}, {"ctx": (ctx + 2) % count}
    barrier = pltpu.get_barrier_semaphore()
    for target in (to_x, to_y, to_core):
        pl.semaphore_signal(barrier, inc=1, device_id=target, device_id_type=MESH)
    for there, target in ((below, to_below), (above, to_above)):
        @pl.when(there)
        def _(target=target):
            pl.semaphore_signal(barrier, inc=1, device_id=target, device_id_type=MESH)

    def greet_all():
        def pass_along(sem, first, then, target):
            @pl.when(first)
            def _():
                pl.semaphore_wait(sem, 1)

            @pl.when(then)
            def _():
                pl.semaphore_signal(sem, inc=1, device_id=target, device_id_type=MESH)

        @pl.when(chip >= chips // 2)
        def _():
            pass_along(greet_down, above, below, to_below)
        pass_along(greet_up, below, above, to_above)

        @pl.when(chip < chips // 2)
        def _():
            pass_along(greet_down, above, below, to_below)

    my_rows = pl.ds(pl.multiple_of(core * length, length), length)
    my_heads = pl.ds(pl.multiple_of(core * nh, nh), nh)
    their_heads = pl.ds(pl.multiple_of((1 - core) * nh, nh), nh)
    my_lams = pl.ds(pl.multiple_of(core * lams, 16), lams)
    my_cols = pl.ds(pl.multiple_of(core * nh * head_dim, LANES), nh * head_dim)

    def head_cols(h):
        return pl.ds(pl.multiple_of((core * nh + h) * head_dim, LANES), head_dim)

    local = [
        pltpu.make_async_copy(decay_ref.at[my_heads], dec.at[my_heads], load_sem.at[0]),
        pltpu.make_async_copy(x_ref, xs.at[my_rows], load_sem.at[1]),
        pltpu.make_async_copy(q_ref, big_q.at[3], load_sem.at[2]),
        pltpu.make_async_copy(k_ref, big_k.at[3], load_sem.at[3]),
        pltpu.make_async_copy(lam_t_ref.at[my_lams], big_l.at[3], load_sem.at[4]),
        pltpu.make_async_copy(gain_hbm, gain_ref, load_sem.at[5]),
    ] + [pltpu.make_async_copy(v_ref.at[:, head_cols(h)], big_v.at[h, 3], load_sem.at[6])
         for h in range(nh)]

    half = depth // 2
    cut = min(lams, CUT)
    lam_parts = [(0, cut)] + ([(cut, lams)] if cut < lams else [])
    pieces = [(k_ref, None, big_k, core * half, core * half, half),
              (q_ref, None, big_q, core * half, core * half, half),
              (lam_t_ref, None, big_l, core * lams, 0, cut)]
    parts = []
    for h in range(nh):
        size = depth // (LAST_PARTS if h == nh - 1 else 1)
        parts.append(range(len(pieces), len(pieces) + depth // size))
        pieces += [(v_ref, head_cols(h), big_v.at[h], low, low, size)
                   for low in range(0, depth, size)]
    pieces += [(lam_t_ref, None, big_l, core * lams + low, low, high - low)
               for low, high in lam_parts[1:]]
    total = len(pieces)
    weight = [piece[5] * (depth if piece[0] is lam_t_ref else head_dim) / (depth * head_dim)
              for piece in pieces]
    issued = []

    def send_ahead(step):
        while (len(issued) < total
               and sum(weight[step + 1:len(issued) + 1]) <= AHEAD):
            send_own(len(issued))
            issued.append(step)

    share = [SHARE_FIRST] * 3 + [SHARE] * (total - 3)
    share[total - len(SHARE_LATE):] = SHARE_LATE

    def shares(i):
        n = pieces[i][5]
        first = (n // 2 + 15) // 16 * 16
        shared = min(int(n * share[i] / 16 + 0.5) * 16, n - first)
        return shared, n - shared, first

    def rows_at(base, start, size):
        return pl.ds(pl.multiple_of(base + start, 16), size)

    def direct_start(way, shared):
        return (1 - side if way else side) * shared

    def send_own(i):
        src, cols, buf, src_base, base, n = pieces[i]
        shared, direct, first = shares(i)
        for way, target in enumerate((to_x, to_y)):
            start = direct_start(way, shared)
            rows = rows_at(src_base, start, direct)
            remote(src.at[rows] if cols is None else src.at[rows, cols],
                   buf.at[way, rows_at(base, start, direct)],
                   piece_send.at[i], own_recv.at[i], target)

    def relays(i):
        src, cols, buf, src_base, base, n = pieces[i]
        shared, direct, first = shares(i)
        return ((0, to_y, rows_at(base, side * (n - first), first)),
                (1, to_x, rows_at(base, (1 - side) * first, n - first)))

    def relay(i):
        src, cols, buf, src_base, base, n = pieces[i]
        shared, direct, first = shares(i)
        await_at(buf.at[pl.ds(0, 2), pl.ds(0, direct)], own_recv.at[i])
        for way, target, rows in relays(i):
            remote(buf.at[way, rows], buf.at[2, rows], piece_send.at[i], cross_recv.at[i], target)
        if shared > 0:
            for way in range(2):
                rows = rows_at(base, (1 - side if way else side) * direct, shared)
                remote(buf.at[way, rows], buf.at[way, rows], piece_send.at[i],
                       cross_recv.at[i], to_z)

    def crossed(i):
        src, cols, buf, src_base, base, n = pieces[i]
        shared, direct, first = shares(i)
        await_at(buf.at[pl.ds(0, 2), pl.ds(0, n // 2 + shared)], cross_recv.at[i])
        if i < 2:
            spot = buf.at[pl.ds(0, 3), rows_at(base, 0, n)]
            remote(spot, spot, core_send.at[i], core_recv.at[i], to_core)

    def own_part(way, low=0, size=depth):
        return pl.ds(pl.multiple_of(owners[way] * depth + low, LANES), size)

    plain = (((1,), (0,)), ((), ()))
    turned = (((1,), (1,)), ((), ()))

    def gathered(weights, dims, ways=(3, 0, 1, 2), acc=None):
        for way in ways:
            term = lax.dot_general(
                xs[:, own_part(way)], weights(way), dims, preferred_element_type=f32)
            acc = term if acc is None else acc + term
        return acc

    def task_k():
        await_at(big_k.at[pl.ds(0, 3), rows_at((1 - core) * half, 0, half)], core_recv.at[0])
        keys = gathered(lambda way: big_k[way], plain).astype(bf16)
        qk[:, state_dim:] = keys
        keys_t[...] = keys.astype(f32).T

    def task_q():
        await_at(big_q.at[pl.ds(0, 3), rows_at((1 - core) * half, 0, half)], core_recv.at[1])
        qk[:, :state_dim] = gathered(lambda way: big_q[way], plain).astype(bf16)
        row = lax.broadcasted_iota(jnp.int32, (length, length), 0)
        col = lax.broadcasted_iota(jnp.int32, (length, length), 1)
        for blk in range(2):
            rows = slice(blk * length, (blk + 1) * length)
            full = lax.dot_general(
                qk[rows, :state_dim], qk[rows, state_dim:], turned, preferred_element_type=f32)
            score[blk] = jnp.where(row >= col, full * scale, 0.0)

    def task_lam(part):
        low, high = lam_parts[part]
        lam[part, :, :high - low] = jax.nn.softplus(
            gathered(lambda way: big_l[way, low:high], turned))

    def lam_at(rows, at):
        part = 0 if at < cut else 1
        at -= part * cut
        return lam[part, rows, at:at + 1]

    def task_early(h):
        mixed[h] = gathered(lambda way: big_v[h, way], plain, (3,))

    def task_sums():
        row = lax.broadcasted_iota(jnp.int32, (length, length), 0)
        col = lax.broadcasted_iota(jnp.int32, (length, length), 1)
        below = (row >= col).astype(f32)
        decays = dec[...]
        ones = jnp.ones((length, LANES), f32)
        sums = jnp.dot(decays, ones, precision=HIGHEST, preferred_element_type=f32)
        logs[0] = sums[:nh] + sums[nh:]
        coef[0, 0] = jnp.exp(sums[nh:])
        for r in range(1, chips):
            remote(logs.at[0], logs.at[r], log_send.at[0], log_recv.at[0], peers[r])
        cum_col = lax.dot_general(
            below, decays, turned, precision=HIGHEST, preferred_element_type=f32)
        cum_row = lax.dot_general(
            decays, below, turned, precision=HIGHEST, preferred_element_type=f32)
        cum_rows[...] = cum_row
        moved = jnp.concatenate((jnp.zeros((nh, length), f32), decays[:nh]), axis=0)
        before = lax.dot_general(
            jnp.ones((length, length), f32), moved, turned, precision=HIGHEST,
            preferred_element_type=f32)
        cum_cols[...] = cum_col
        grow[...] = jnp.exp(cum_col) * scale
        reach_grow[...] = jnp.exp(cum_col + before) * scale
        remain[...] = jnp.exp(cum_row[:, length - 1:length] - cum_row)

    def task_coef():
        if chips > 1:
            await_at(logs.at[pl.ds(1, chips - 1)], log_recv.at[0])
        own_log = logs[0]
        carry_log = jnp.zeros_like(own_log)
        for b in range(1, bits):
            upper = ((ctx // (1 << b)) % 2).astype(f32)
            step = 1 << (b - 1)
            other = logs[step]
            for r in range(step + 1, 2 * step):
                other = other + logs[r]
            coef[b, 0] = jnp.exp(carry_log) * upper
            coef[b, 1] = jnp.where(upper > 0, 1.0, jnp.exp(other))
            coef[b, 2] = jnp.where(upper > 0, jnp.exp(own_log), 1.0)
            if b == bits - 1 and b > 1:
                same = logs[step]
                for r in range(step + 1, step + step // 2):
                    same = same + logs[r]
                odd = ((ctx // (1 << (b - 1))) % 2).astype(f32)
                late = jnp.exp(jnp.where(odd > 0, same, other - same))
                coef[b, 3] = jnp.where(odd > 0, 1.0, late)
                coef[b, 4] = jnp.where(odd > 0, late, 1.0)
            carry_log = carry_log + upper * other
            own_log = own_log + other

    def upper_at(b):
        return (ctx // (1 << b)) % 2 == 1

    def merges_at(b):
        return ctx // (2 << b) != count // (2 << b) - 1

    def state_copy(h, b):
        return pltpu.make_async_remote_copy(
            src_ref=sent.at[b, h], dst_ref=got.at[b, h], send_sem=st_send.at[b],
            recv_sem=st_recv.at[b, h], device_id=peers[1 << (b - 1)], device_id_type=MESH)

    def sends_at(b):
        return jnp.logical_or(jnp.logical_not(upper_at(b)), merges_at(b))

    def takes_at(b):
        return jnp.logical_or(upper_at(b), merges_at(b))

    top, mid = bits - 1, bits - 2

    def is_direct(h):
        return bits > 2 and h >= nh - DIRECT

    def send_direct(h):
        source = sent.at[mid, h]

        @pl.when(jnp.logical_not(upper_at(mid)))
        def _():
            remote(source, got.at[mid, h], direct_send.at[0], st_recv.at[mid, h],
                   peers[1 << (mid - 1)])

        @pl.when(jnp.logical_not(upper_at(top)))
        def _():
            remote(source, got.at[top, h], direct_send.at[1], st_recv.at[top, h],
                   peers[1 << (top - 1)])
            remote(source, got_far.at[h], direct_send.at[1], st_recv.at[top, h],
                   peers[3 << (mid - 1)])

    def send_state(h, b):
        if is_direct(h) and b == mid:
            send_direct(h)
            return

        @pl.when(sends_at(b))
        def _():
            state_copy(h, b).start()

    def await_state(h, b):
        @pl.when(takes_at(b))
        def _():
            await_at(got.at[b, h], st_recv.at[b, h])

    def add_part(h, p):
        low, size = pieces[parts[h][p]][4:]
        acc = mixed[h]
        for way in range(3):
            acc = acc + jnp.dot(
                xs[:, own_part(way, low, size)], big_v[h, way, low:low + size],
                preferred_element_type=f32)
        return acc

    def task_part(h, p):
        mixed[h] = add_part(h, p)

    def task_head(h):
        val[h] = add_part(h, len(parts[h]) - 1).astype(bf16)
        blocks = []
        for blk in range(2):
            rows = slice(blk * length, (blk + 1) * length)
            at = blk * nh + h
            keyed = (keys_t[:, rows] * remain[at:at + 1]).astype(bf16)
            blocks.append(jnp.dot(keyed, val[h, rows], preferred_element_type=f32))
        sent[0, h] = blocks[0].astype(bf16)
        if bits > 1:
            whole = coef[0, 0, h:h + 1] * blocks[0] + blocks[1]
            state[h] = whole
            sent[1, h] = whole.astype(bf16)
            send_state(h, 1)

    tile = 128
    tiles = length // tile

    def task_near(h, blk):
        trow = lax.broadcasted_iota(jnp.int32, (tile, tile), 0)
        tcol = lax.broadcasted_iota(jnp.int32, (tile, tile), 1)
        differ = jnp.bitwise_xor(trow, tcol)
        deep = tile.bit_length() - 1
        base = h * levels
        at_cum = blk * nh + h
        low = blk * length
        for ti in range(tiles):
            rows = slice(low + ti * tile, low + (ti + 1) * tile)
            here = slice(ti * tile, (ti + 1) * tile)
            acc = None
            for tj in range(ti + 1):
                cols = slice(tj * tile, (tj + 1) * tile)
                if ti == tj:
                    weight = jnp.broadcast_to(lam_at(rows, base), (tile, tile))
                    for level in range(1, deep + 1):
                        at = base + level
                        weight = jnp.where(
                            differ >= 1 << (level - 1), lam_at(rows, at), weight)
                else:
                    at = base + deep + (ti ^ tj).bit_length()
                    weight = lam_at(rows, at)
                distance = cum_cols[here, at_cum:at_cum + 1] - cum_rows[at_cum:at_cum + 1, cols]
                decay = jnp.exp(jnp.minimum(distance, 0.0))
                mix = (weight * (decay * score[blk, here, cols])).astype(bf16)
                term = jnp.dot(
                    mix, val[h, low + tj * tile:low + (tj + 1) * tile],
                    preferred_element_type=f32)
                acc = term if acc is None else acc + term
            if blk == 1:
                reach = jnp.dot(qk[rows, :state_dim], sent[0, h], preferred_element_type=f32)
                at = base + inner
                acc = acc + lam_at(rows, at) * grow[here, at_cum:at_cum + 1] * reach
            mixed[h, rows] = acc

    def far(h, b):
        other = got[b, h].astype(f32)
        if is_direct(h) and b == top:
            other = coef[b, 3, h:h + 1] * other + coef[b, 4, h:h + 1] * got_far[h].astype(f32)
        carried = (coef[b, 0, h:h + 1] * other).astype(bf16)
        reach = jnp.dot(qk[:, :state_dim], carried, preferred_element_type=f32)
        at = h * levels + inner + b
        grown = jnp.concatenate((reach_grow[:, h:h + 1], reach_grow[:, nh + h:nh + h + 1]), axis=0)
        return lam_at(slice(None), at) * grown * reach

    def task_merge(h, b):
        await_state(h, b)

        @pl.when(merges_at(b))
        def _():
            block = coef[b, 1, h:h + 1] * state[h] + coef[b, 2, h:h + 1] * got[b, h].astype(f32)
            state[h] = block
            sent[b + 1, h] = block.astype(bf16)
        send_state(h, b + 1)

    def task_far(h, b):
        @pl.when(upper_at(b))
        def _():
            if is_direct(h) and b >= mid:
                await_at(got.at[pl.ds(0, 1 + (b == top)), h], st_recv.at[b, h])
            mixed[h] += far(h, b)

    def task_finish(h):
        if bits > 1:
            if not is_direct(h):
                await_state(h, top)
            task_far(h, top)
        whole = mixed[h]
        mean_square = jnp.mean(whole * whole, axis=-1, keepdims=True)
        gain = gain_ref[:, head_cols(h)]
        result[h] = (whole * lax.rsqrt(mean_square + 1e-05) * gain).astype(bf16)
        remote(result.at[h, pl.ds(pl.multiple_of((1 - core) * length, length), length)],
               out_ref.at[:, head_cols(h)], give_send.at[0], give_recv.at[0], to_core)
        pltpu.make_async_copy(
            result.at[h, my_rows], out_ref.at[:, head_cols(h)], out_sem.at[0]).start()

    for copy in local:
        copy.start()
    pl.semaphore_wait(barrier, 3 + below.astype(jnp.int32) + above.astype(jnp.int32))
    send_ahead(-1)
    remote(decay_ref.at[their_heads], dec.at[my_heads], swap_send.at[0], swap_recv.at[0], to_core)
    remote(x_ref, xs.at[my_rows], swap_send.at[1], swap_recv.at[1], to_core)
    greet_all()

    def task_loads():
        for copy in local[1:6]:
            copy.wait()
        await_at(big_v.at[:, 3], load_sem.at[6])
        await_at(
            xs.at[pl.ds(pl.multiple_of((1 - core) * length, length), length)], swap_recv.at[1])

    def task_decays():
        local[0].wait()
        await_at(dec.at[their_heads], swap_recv.at[0])
        task_sums()

    def task_output(h):
        task_finish(h)

    def call(task, *what):
        return functools.partial(task, *what)

    tasks = {}
    final = total

    def plan(step, rank, task, *what):
        tasks.setdefault(min(step, final), []).append((rank, call(task, *what)))

    plan(0, 0, task_decays)
    plan(0, 0, task_loads)
    for h in range(nh):
        plan(h // 3, 0, task_early, h)
    plan(2, 0, task_coef)
    plan(2, 1, task_k)
    plan(3, 0, task_q)
    plan(3, 1, task_lam, 0)
    for p in range(1, len(lam_parts)):
        plan(final, 2, task_lam, p)
    for h in range(nh):
        at = parts[h][-1] + 1
        left = nh - 1 - h
        for p in range(len(parts[h]) - 1):
            plan(parts[h][p] + 1, 0, task_part, h, p)
        plan(at, 1, task_head, h)
        merged = at + 1 + (left == 2)
        near = (at + 1, at + 1) if left > 2 else (at + 2, at + 3) if left == 2 else (final, final)
        if (h + 1) * levels > cut:
            near = (final, final)
        for b in range(1, mid if is_direct(h) else top):
            plan(final - 1 if left == 1 else merged, 3, task_merge, h, b)
        for b in range(1, top):
            plan(near[1], 8 if left == 0 else 6, task_far, h, b)
        for blk in range(2):
            plan(near[blk], 5, task_near, h, blk)
        if left > 2:
            plan(at + 2 + (left == 3), 4, task_output, h)
        else:
            plan(final - 1 if left == 2 else final, 9 if left == 0 else 7, task_output, h)
    for step in range(total + 1):
        if step < total:
            relay(step)
            send_ahead(step)
        if step >= 1:
            crossed(step - 1)
        for rank, task in sorted(tasks.pop(step, []), key=lambda entry: entry[0]):
            task()
    for b in range(1, bits):
        heads_at = nh - (DIRECT if bits > 2 and b >= mid else 0)

        @pl.when(sends_at(b))
        def _(b=b, heads_at=heads_at):
            await_at(sent.at[b, pl.ds(0, heads_at)], st_send.at[b])
    if bits > 2 and DIRECT:
        @pl.when(jnp.logical_not(upper_at(mid)))
        def _():
            await_at(sent.at[0, pl.ds(0, DIRECT)], direct_send.at[0])

        @pl.when(jnp.logical_not(upper_at(top)))
        def _():
            await_at(sent.at[pl.ds(0, 2), pl.ds(0, DIRECT)], direct_send.at[1])
    await_at(dec.at[their_heads], swap_send.at[0])
    await_at(xs.at[my_rows], swap_send.at[1])
    for i in range(total):
        src, cols, buf, src_base, base, n = pieces[i]
        await_at(buf.at[pl.ds(0, 3), pl.ds(0, n)], piece_send.at[i])
    for i in range(2):
        await_at(pieces[i][2].at[pl.ds(0, 3), pl.ds(0, half)], core_send.at[i])
    if chips > 1:
        await_at(logs.at[pl.ds(1, chips - 1)], log_send.at[0])
    await_at(out_ref.at[:, my_cols], out_sem.at[0])
    await_at(out_ref.at[:, my_cols], give_send.at[0])
    their_cols = pl.ds(pl.multiple_of((1 - core) * nh * head_dim, LANES), nh * head_dim)
    await_at(out_ref.at[:, their_cols], give_recv.at[0])


def per_device(inputs, query_weight, key_weight, value_weight, lambda_weight, log_decay, norm_gain):
    count = lax.axis_size("ctx")
    chips = count // 2
    bits = count.bit_length() - 1
    length, width = inputs.shape[1:]
    depth, wide = value_weight.shape
    heads = log_decay.shape[2]
    levels = lambda_weight.shape[1] // heads
    state_dim = query_weight.shape[1]
    head_dim = wide // heads
    nh = heads // 2
    lams = lambda_weight.shape[1] // 2
    total = 3 + nh - 1 + LAST_PARTS + (1 if lams > CUT else 0)
    f32, bf16 = jnp.float32, jnp.bfloat16
    anywhere = pl.BlockSpec(memory_space=pl.ANY)
    dma = pltpu.SemaphoreType.DMA
    out = pl.pallas_call(
        functools.partial(fused_kernel, levels),
        out_shape=pltpu.VMEM((length, wide), bf16),
        in_specs=[anywhere] * 7,
        out_specs=anywhere,
        scratch_shapes=[
            pltpu.VMEM((1, wide), f32),
            pltpu.VMEM((2 * length, width), bf16),
            pltpu.VMEM((2 * nh, length), f32),
            pltpu.VMEM((4, depth, state_dim), bf16),
            pltpu.VMEM((4, depth, state_dim), bf16),
            pltpu.VMEM((4, lams, depth), bf16),
            pltpu.VMEM((nh, 4, depth, head_dim), bf16),
            pltpu.VMEM((2 * length, 2 * state_dim), bf16),
            pltpu.VMEM((2, 2 * length, -(-max(CUT, lams - CUT) // LANES) * LANES), f32),
            pltpu.VMEM((nh, 2 * length, head_dim), bf16),
            pltpu.VMEM((2, length, length), f32),
            pltpu.VMEM((2 * nh, length), f32),
            pltpu.VMEM((length, 2 * nh), f32),
            pltpu.VMEM((length, 2 * nh), f32),
            pltpu.VMEM((length, 2 * nh), f32),
            pltpu.VMEM((2 * nh, length), f32),
            pltpu.VMEM((state_dim, 2 * length), f32),
            pltpu.VMEM((chips, nh, LANES), f32),
            pltpu.VMEM((bits, 5, nh, LANES), f32),
            pltpu.VMEM((nh, state_dim, head_dim), f32),
            pltpu.VMEM((bits, nh, state_dim, head_dim), bf16),
            pltpu.VMEM((bits, nh, state_dim, head_dim), bf16),
            pltpu.VMEM((nh, state_dim, head_dim), bf16),
            pltpu.VMEM((nh, 2 * length, head_dim), f32),
            pltpu.VMEM((nh, 2 * length, head_dim), bf16),
            dma((7,)),
            dma((2,)),
            dma((2,)),
            dma((total,)),
            dma((total,)),
            dma((total,)),
            dma((2,)),
            dma((2,)),
            dma((1,)),
            dma((1,)),
            dma((bits,)),
            dma((bits, nh)),
            dma((2,)),
            dma((1,)),
            dma((1,)),
            dma((1,)),
            pltpu.SemaphoreType.REGULAR,
            pltpu.SemaphoreType.REGULAR,
        ],
        compiler_params=pltpu.CompilerParams(
            collective_id=0, has_side_effects=True, vmem_limit_bytes=VMEM_LIMIT),
        name="gather_mix",
    )(inputs[0], query_weight, key_weight, lambda_weight.T, value_weight, log_decay[0].T,
      norm_gain[None])
    return out[None]


def solution(mesh):
    return jax.shard_map(
        per_device,
        mesh=mesh,
        in_specs=(
            P("dp", "ctx", None),
            P("dp", None),
            P("dp", None),
            P("dp", None),
            P("dp", None),
            P("dp", "ctx", None),
            P(),
        ),
        out_specs=P("dp", "ctx", None),
        check_vma=False,
    )
```

```python
import functools
import math

import jax
import jax.numpy as jnp
from jax import lax
from jax.experimental import pallas as pl
from jax.experimental.pallas import tpu as pltpu
from jax.sharding import PartitionSpec as P

HIGHEST = lax.Precision.HIGHEST
MESH = pl.DeviceIdType.MESH
VMEM_LIMIT = 60 * 1024 * 1024

AHEAD = 2.0
SHARE = 6.5 / 16
SHARE_FIRST = 8 / 16
SHARE_LATE = (8/16,)*2
CUT = 160
LAST_PARTS = 2
DIRECT = 1
LANES = 128


def flipped(index, mask):
    out = index
    for power in range(mask.bit_length()):
        if mask >> power & 1:
            step = 1 << power
            out = out + step - 2 * step * ((index // step) % 2)
    return out


def fused_kernel(levels, x_ref, q_ref, k_ref, lam_t_ref, v_ref, decay_ref, gain_hbm, out_ref,
                 gain_ref, xs, dec, big_q, big_k, big_l, big_v, qk, lam, val, score, cum_rows, cum_cols,
                 grow, reach_grow, remain, keys_t, logs, coef, state, sent, got, got_far, mixed, result,
                 load_sem, swap_send, swap_recv, own_recv, cross_recv, piece_send, core_send,
                 core_recv, log_send, log_recv, st_send, st_recv, direct_send, out_sem,
                 give_send, give_recv, greet_up, greet_down):
    f32, bf16 = jnp.float32, jnp.bfloat16
    count = lax.axis_size("ctx")
    chips = count // 2
    bits = count.bit_length() - 1
    dp = lax.axis_index("dp")
    ctx = lax.axis_index("ctx")
    x_at, y_at = dp % 2, dp // 2
    core = ctx % 2
    side = (ctx // 2) % 2
    length = x_ref.shape[0]
    depth, wide = v_ref.shape
    nh = decay_ref.shape[0] // 2
    lams = lam_t_ref.shape[0] // 2
    head_dim = wide // (2 * nh)
    state_dim = q_ref.shape[1]
    inner = length.bit_length()
    scale = 1.0 / math.sqrt(state_dim)
    to_x = {"dp": y_at * 2 + (1 - x_at)}
    to_y = {"dp": (1 - y_at) * 2 + x_at}
    to_core = {"ctx": flipped(ctx, 1)}
    to_z = {"ctx": flipped(ctx, 2)}
    peers = [None] + [{"ctx": flipped(ctx, 2 * r)} for r in range(1, chips)]
    owners = (y_at * 2 + (1 - x_at), (1 - y_at) * 2 + x_at, (1 - y_at) * 2 + (1 - x_at), dp)
    def remote(src, dst, out_sem_, in_sem, target):
        pltpu.make_async_remote_copy(
            src_ref=src, dst_ref=dst, send_sem=out_sem_, recv_sem=in_sem,
            device_id=target, device_id_type=MESH).start()

    def await_at(spot, sem):
        pltpu.make_async_copy(spot, spot, sem).wait()

    chip = ctx // 2
    below, above = chip > 0, chip < chips - 1
    to_below, to_above = {"ctx": (ctx + count - 2) % count}, {"ctx": (ctx + 2) % count}
    barrier = pltpu.get_barrier_semaphore()
    for target in (to_x, to_y, to_core):
        pl.semaphore_signal(barrier, inc=1, device_id=target, device_id_type=MESH)
    for there, target in ((below, to_below), (above, to_above)):
        @pl.when(there)
        def _(target=target):
            pl.semaphore_signal(barrier, inc=1, device_id=target, device_id_type=MESH)

    def greet_all():
        def pass_along(sem, first, then, target):
            @pl.when(first)
            def _():
                pl.semaphore_wait(sem, 1)

            @pl.when(then)
            def _():
                pl.semaphore_signal(sem, inc=1, device_id=target, device_id_type=MESH)

        @pl.when(chip >= chips // 2)
        def _():
            pass_along(greet_down, above, below, to_below)
        pass_along(greet_up, below, above, to_above)

        @pl.when(chip < chips // 2)
        def _():
            pass_along(greet_down, above, below, to_below)

    my_rows = pl.ds(pl.multiple_of(core * length, length), length)
    my_heads = pl.ds(pl.multiple_of(core * nh, nh), nh)
    their_heads = pl.ds(pl.multiple_of((1 - core) * nh, nh), nh)
    my_lams = pl.ds(pl.multiple_of(core * lams, 16), lams)
    my_cols = pl.ds(pl.multiple_of(core * nh * head_dim, LANES), nh * head_dim)

    def head_cols(h):
        return pl.ds(pl.multiple_of((core * nh + h) * head_dim, LANES), head_dim)

    local = [
        pltpu.make_async_copy(decay_ref.at[my_heads], dec.at[my_heads], load_sem.at[0]),
        pltpu.make_async_copy(x_ref, xs.at[my_rows], load_sem.at[1]),
        pltpu.make_async_copy(q_ref, big_q.at[3], load_sem.at[2]),
        pltpu.make_async_copy(k_ref, big_k.at[3], load_sem.at[3]),
        pltpu.make_async_copy(lam_t_ref.at[my_lams], big_l.at[3], load_sem.at[4]),
        pltpu.make_async_copy(gain_hbm, gain_ref, load_sem.at[5]),
    ] + [pltpu.make_async_copy(v_ref.at[:, head_cols(h)], big_v.at[h, 3], load_sem.at[6])
         for h in range(nh)]

    half = depth // 2
    cut = min(lams, CUT)
    lam_parts = [(0, cut)] + ([(cut, lams)] if cut < lams else [])
    pieces = [(k_ref, None, big_k, core * half, core * half, half),
              (q_ref, None, big_q, core * half, core * half, half),
              (lam_t_ref, None, big_l, core * lams, 0, cut)]
    parts = []
    for h in range(nh):
        size = depth // (LAST_PARTS if h == nh - 1 else 1)
        parts.append(range(len(pieces), len(pieces) + depth // size))
        pieces += [(v_ref, head_cols(h), big_v.at[h], low, low, size)
                   for low in range(0, depth, size)]
    pieces += [(lam_t_ref, None, big_l, core * lams + low, low, high - low)
               for low, high in lam_parts[1:]]
    total = len(pieces)
    weight = [piece[5] * (depth if piece[0] is lam_t_ref else head_dim) / (depth * head_dim)
              for piece in pieces]
    issued = []

    def send_ahead(step):
        while (len(issued) < total
               and sum(weight[step + 1:len(issued) + 1]) <= AHEAD):
            send_own(len(issued))
            issued.append(step)

    share = [SHARE_FIRST] * 3 + [SHARE] * (total - 3)
    share[total - len(SHARE_LATE):] = SHARE_LATE

    def shares(i):
        n = pieces[i][5]
        first = (n // 2 + 15) // 16 * 16
        shared = min(int(n * share[i] / 16 + 0.5) * 16, n - first)
        return shared, n - shared, first

    def rows_at(base, start, size):
        return pl.ds(pl.multiple_of(base + start, 16), size)

    def direct_start(way, shared):
        return (1 - side if way else side) * shared

    def send_own(i):
        src, cols, buf, src_base, base, n = pieces[i]
        shared, direct, first = shares(i)
        for way, target in enumerate((to_x, to_y)):
            start = direct_start(way, shared)
            rows = rows_at(src_base, start, direct)
            remote(src.at[rows] if cols is None else src.at[rows, cols],
                   buf.at[way, rows_at(base, start, direct)],
                   piece_send.at[i], own_recv.at[i], target)

    def relays(i):
        src, cols, buf, src_base, base, n = pieces[i]
        shared, direct, first = shares(i)
        return ((0, to_y, rows_at(base, side * (n - first), first)),
                (1, to_x, rows_at(base, (1 - side) * first, n - first)))

    def relay(i):
        src, cols, buf, src_base, base, n = pieces[i]
        shared, direct, first = shares(i)
        await_at(buf.at[pl.ds(0, 2), pl.ds(0, direct)], own_recv.at[i])
        for way, target, rows in relays(i):
            remote(buf.at[way, rows], buf.at[2, rows], piece_send.at[i], cross_recv.at[i], target)
        if shared > 0:
            for way in range(2):
                rows = rows_at(base, (1 - side if way else side) * direct, shared)
                remote(buf.at[way, rows], buf.at[way, rows], piece_send.at[i],
                       cross_recv.at[i], to_z)

    def crossed(i):
        src, cols, buf, src_base, base, n = pieces[i]
        shared, direct, first = shares(i)
        await_at(buf.at[pl.ds(0, 2), pl.ds(0, n // 2 + shared)], cross_recv.at[i])
        if i < 2:
            spot = buf.at[pl.ds(0, 3), rows_at(base, 0, n)]
            remote(spot, spot, core_send.at[i], core_recv.at[i], to_core)

    def own_part(way, low=0, size=depth):
        return pl.ds(pl.multiple_of(owners[way] * depth + low, LANES), size)

    plain = (((1,), (0,)), ((), ()))
    turned = (((1,), (1,)), ((), ()))

    def gathered(weights, dims, ways=(3, 0, 1, 2), acc=None):
        for way in ways:
            term = lax.dot_general(
                xs[:, own_part(way)], weights(way), dims, preferred_element_type=f32)
            acc = term if acc is None else acc + term
        return acc

    def task_k():
        await_at(big_k.at[pl.ds(0, 3), rows_at((1 - core) * half, 0, half)], core_recv.at[0])
        keys = gathered(lambda way: big_k[way], plain).astype(bf16)
        qk[:, state_dim:] = keys
        keys_t[...] = keys.astype(f32).T

    def task_q():
        await_at(big_q.at[pl.ds(0, 3), rows_at((1 - core) * half, 0, half)], core_recv.at[1])
        qk[:, :state_dim] = gathered(lambda way: big_q[way], plain).astype(bf16)
        row = lax.broadcasted_iota(jnp.int32, (length, length), 0)
        col = lax.broadcasted_iota(jnp.int32, (length, length), 1)
        for blk in range(2):
            rows = slice(blk * length, (blk + 1) * length)
            full = lax.dot_general(
                qk[rows, :state_dim], qk[rows, state_dim:], turned, preferred_element_type=f32)
            score[blk] = jnp.where(row >= col, full * scale, 0.0)

    def task_lam(part):
        low, high = lam_parts[part]
        lam[part, :, :high - low] = jax.nn.softplus(
            gathered(lambda way: big_l[way, low:high], turned))

    def lam_at(rows, at):
        part = 0 if at < cut else 1
        at -= part * cut
        return lam[part, rows, at:at + 1]

    def task_early(h):
        mixed[h] = gathered(lambda way: big_v[h, way], plain, (3,))

    def task_sums():
        row = lax.broadcasted_iota(jnp.int32, (length, length), 0)
        col = lax.broadcasted_iota(jnp.int32, (length, length), 1)
        below = (row >= col).astype(f32)
        decays = dec[...]
        ones = jnp.ones((length, LANES), f32)
        sums = jnp.dot(decays, ones, precision=HIGHEST, preferred_element_type=f32)
        logs[0] = sums[:nh] + sums[nh:]
        coef[0, 0] = jnp.exp(sums[nh:])
        for r in range(1, chips):
            remote(logs.at[0], logs.at[r], log_send.at[0], log_recv.at[0], peers[r])
        cum_col = lax.dot_general(
            below, decays, turned, precision=HIGHEST, preferred_element_type=f32)
        cum_row = lax.dot_general(
            decays, below, turned, precision=HIGHEST, preferred_element_type=f32)
        cum_rows[...] = cum_row
        moved = jnp.concatenate((jnp.zeros((nh, length), f32), decays[:nh]), axis=0)
        before = lax.dot_general(
            jnp.ones((length, length), f32), moved, turned, precision=HIGHEST,
            preferred_element_type=f32)
        cum_cols[...] = cum_col
        grow[...] = jnp.exp(cum_col) * scale
        reach_grow[...] = jnp.exp(cum_col + before) * scale
        remain[...] = jnp.exp(cum_row[:, length - 1:length] - cum_row)

    def task_coef():
        if chips > 1:
            await_at(logs.at[pl.ds(1, chips - 1)], log_recv.at[0])
        own_log = logs[0]
        carry_log = jnp.zeros_like(own_log)
        for b in range(1, bits):
            upper = ((ctx // (1 << b)) % 2).astype(f32)
            step = 1 << (b - 1)
            other = logs[step]
            for r in range(step + 1, 2 * step):
                other = other + logs[r]
            coef[b, 0] = jnp.exp(carry_log) * upper
            coef[b, 1] = jnp.where(upper > 0, 1.0, jnp.exp(other))
            coef[b, 2] = jnp.where(upper > 0, jnp.exp(own_log), 1.0)
            if b == bits - 1 and b > 1:
                same = logs[step]
                for r in range(step + 1, step + step // 2):
                    same = same + logs[r]
                odd = ((ctx // (1 << (b - 1))) % 2).astype(f32)
                late = jnp.exp(jnp.where(odd > 0, same, other - same))
                coef[b, 3] = jnp.where(odd > 0, 1.0, late)
                coef[b, 4] = jnp.where(odd > 0, late, 1.0)
            carry_log = carry_log + upper * other
            own_log = own_log + other

    def upper_at(b):
        return (ctx // (1 << b)) % 2 == 1

    def merges_at(b):
        return ctx // (2 << b) != count // (2 << b) - 1

    def state_copy(h, b):
        return pltpu.make_async_remote_copy(
            src_ref=sent.at[b, h], dst_ref=got.at[b, h], send_sem=st_send.at[b],
            recv_sem=st_recv.at[b, h], device_id=peers[1 << (b - 1)], device_id_type=MESH)

    def sends_at(b):
        return jnp.logical_or(jnp.logical_not(upper_at(b)), merges_at(b))

    def takes_at(b):
        return jnp.logical_or(upper_at(b), merges_at(b))

    top, mid = bits - 1, bits - 2

    def is_direct(h):
        return bits > 2 and h >= nh - DIRECT

    def send_direct(h):
        source = sent.at[mid, h]

        @pl.when(jnp.logical_not(upper_at(mid)))
        def _():
            remote(source, got.at[mid, h], direct_send.at[0], st_recv.at[mid, h],
                   peers[1 << (mid - 1)])

        @pl.when(jnp.logical_not(upper_at(top)))
        def _():
            remote(source, got.at[top, h], direct_send.at[1], st_recv.at[top, h],
                   peers[1 << (top - 1)])
            remote(source, got_far.at[h], direct_send.at[1], st_recv.at[top, h],
                   peers[3 << (mid - 1)])

    def send_state(h, b):
        if is_direct(h) and b == mid:
            send_direct(h)
            return

        @pl.when(sends_at(b))
        def _():
            state_copy(h, b).start()

    def await_state(h, b):
        @pl.when(takes_at(b))
        def _():
            await_at(got.at[b, h], st_recv.at[b, h])

    def add_part(h, p):
        low, size = pieces[parts[h][p]][4:]
        acc = mixed[h]
        for way in range(3):
            acc = acc + jnp.dot(
                xs[:, own_part(way, low, size)], big_v[h, way, low:low + size],
                preferred_element_type=f32)
        return acc

    def task_part(h, p):
        mixed[h] = add_part(h, p)

    def task_head(h):
        val[h] = add_part(h, len(parts[h]) - 1).astype(bf16)
        blocks = []
        for blk in range(2):
            rows = slice(blk * length, (blk + 1) * length)
            at = blk * nh + h
            keyed = (keys_t[:, rows] * remain[at:at + 1]).astype(bf16)
            blocks.append(jnp.dot(keyed, val[h, rows], preferred_element_type=f32))
        sent[0, h] = blocks[0].astype(bf16)
        if bits > 1:
            whole = coef[0, 0, h:h + 1] * blocks[0] + blocks[1]
            state[h] = whole
            sent[1, h] = whole.astype(bf16)
            send_state(h, 1)

    tile = 128
    tiles = length // tile

    def task_near(h, blk):
        trow = lax.broadcasted_iota(jnp.int32, (tile, tile), 0)
        tcol = lax.broadcasted_iota(jnp.int32, (tile, tile), 1)
        differ = jnp.bitwise_xor(trow, tcol)
        deep = tile.bit_length() - 1
        base = h * levels
        at_cum = blk * nh + h
        low = blk * length
        for ti in range(tiles):
            rows = slice(low + ti * tile, low + (ti + 1) * tile)
            here = slice(ti * tile, (ti + 1) * tile)
            acc = None
            for tj in range(ti + 1):
                cols = slice(tj * tile, (tj + 1) * tile)
                if ti == tj:
                    weight = jnp.broadcast_to(lam_at(rows, base), (tile, tile))
                    for level in range(1, deep + 1):
                        at = base + level
                        weight = jnp.where(
                            differ >= 1 << (level - 1), lam_at(rows, at), weight)
                else:
                    at = base + deep + (ti ^ tj).bit_length()
                    weight = lam_at(rows, at)
                distance = cum_cols[here, at_cum:at_cum + 1] - cum_rows[at_cum:at_cum + 1, cols]
                decay = jnp.exp(jnp.minimum(distance, 0.0))
                mix = (weight * (decay * score[blk, here, cols])).astype(bf16)
                term = jnp.dot(
                    mix, val[h, low + tj * tile:low + (tj + 1) * tile],
                    preferred_element_type=f32)
                acc = term if acc is None else acc + term
            if blk == 1:
                reach = jnp.dot(qk[rows, :state_dim], sent[0, h], preferred_element_type=f32)
                at = base + inner
                acc = acc + lam_at(rows, at) * grow[here, at_cum:at_cum + 1] * reach
            mixed[h, rows] = acc

    def far(h, b):
        other = got[b, h].astype(f32)
        if is_direct(h) and b == top:
            other = coef[b, 3, h:h + 1] * other + coef[b, 4, h:h + 1] * got_far[h].astype(f32)
        carried = (coef[b, 0, h:h + 1] * other).astype(bf16)
        reach = jnp.dot(qk[:, :state_dim], carried, preferred_element_type=f32)
        at = h * levels + inner + b
        grown = jnp.concatenate((reach_grow[:, h:h + 1], reach_grow[:, nh + h:nh + h + 1]), axis=0)
        return lam_at(slice(None), at) * grown * reach

    def task_merge(h, b):
        await_state(h, b)

        @pl.when(merges_at(b))
        def _():
            block = coef[b, 1, h:h + 1] * state[h] + coef[b, 2, h:h + 1] * got[b, h].astype(f32)
            state[h] = block
            sent[b + 1, h] = block.astype(bf16)
        send_state(h, b + 1)

    def task_far(h, b):
        @pl.when(upper_at(b))
        def _():
            if is_direct(h) and b >= mid:
                await_at(got.at[pl.ds(0, 1 + (b == top)), h], st_recv.at[b, h])
            mixed[h] += far(h, b)

    def task_finish(h):
        if bits > 1:
            if not is_direct(h):
                await_state(h, top)
            task_far(h, top)
        whole = mixed[h]
        mean_square = jnp.mean(whole * whole, axis=-1, keepdims=True)
        gain = gain_ref[:, head_cols(h)]
        result[h] = (whole * lax.rsqrt(mean_square + 1e-05) * gain).astype(bf16)
        remote(result.at[h, pl.ds(pl.multiple_of((1 - core) * length, length), length)],
               out_ref.at[:, head_cols(h)], give_send.at[0], give_recv.at[0], to_core)
        pltpu.make_async_copy(
            result.at[h, my_rows], out_ref.at[:, head_cols(h)], out_sem.at[0]).start()

    for copy in local:
        copy.start()
    pl.semaphore_wait(barrier, 3 + below.astype(jnp.int32) + above.astype(jnp.int32))
    send_ahead(-1)
    remote(decay_ref.at[their_heads], dec.at[my_heads], swap_send.at[0], swap_recv.at[0], to_core)
    remote(x_ref, xs.at[my_rows], swap_send.at[1], swap_recv.at[1], to_core)
    greet_all()

    def task_loads():
        for copy in local[1:6]:
            copy.wait()
        await_at(big_v.at[:, 3], load_sem.at[6])
        await_at(
            xs.at[pl.ds(pl.multiple_of((1 - core) * length, length), length)], swap_recv.at[1])

    def task_decays():
        local[0].wait()
        await_at(dec.at[their_heads], swap_recv.at[0])
        task_sums()

    def task_output(h):
        task_finish(h)

    def call(task, *what):
        return functools.partial(task, *what)

    tasks = {}
    final = total

    def plan(step, rank, task, *what):
        tasks.setdefault(min(step, final), []).append((rank, call(task, *what)))

    plan(1, 0, task_decays)
    plan(2, 0, task_loads)
    for h in range(nh):
        plan(2 + h // 3, 2, task_early, h)
    plan(3, 0, task_coef)
    plan(2, 1, task_k)
    plan(3, 0, task_q)
    plan(3, 1, task_lam, 0)
    for p in range(1, len(lam_parts)):
        plan(final, 2, task_lam, p)
    for h in range(nh):
        at = parts[h][-1] + 1
        left = nh - 1 - h
        for p in range(len(parts[h]) - 1):
            plan(parts[h][p] + 1, 0, task_part, h, p)
        plan(at, 1, task_head, h)
        merged = at + 1
        near = (at + 1, at + 1)
        if (h + 1) * levels > cut:
            near = (final, final)
        for b in range(1, mid if is_direct(h) else top):
            plan(final - 1 if left == 1 else merged, 3, task_merge, h, b)
        for b in range(1, top):
            plan(near[1], 8 if left == 0 else 6, task_far, h, b)
        for blk in range(2):
            plan(near[blk], 5, task_near, h, blk)
        if left > 2:
            plan(at + 2, 4, task_output, h)
        else:
            plan(final - 1 if left == 2 else final, 9 if left == 0 else 7, task_output, h)
    for step in range(total + 1):
        if step < total:
            relay(step)
            send_ahead(step)
        if step >= 1:
            crossed(step - 1)
        for rank, task in sorted(tasks.pop(step, []), key=lambda entry: entry[0]):
            task()
    for b in range(1, bits):
        heads_at = nh - (DIRECT if bits > 2 and b >= mid else 0)

        @pl.when(sends_at(b))
        def _(b=b, heads_at=heads_at):
            await_at(sent.at[b, pl.ds(0, heads_at)], st_send.at[b])
    if bits > 2 and DIRECT:
        @pl.when(jnp.logical_not(upper_at(mid)))
        def _():
            await_at(sent.at[0, pl.ds(0, DIRECT)], direct_send.at[0])

        @pl.when(jnp.logical_not(upper_at(top)))
        def _():
            await_at(sent.at[pl.ds(0, 2), pl.ds(0, DIRECT)], direct_send.at[1])
    await_at(dec.at[their_heads], swap_send.at[0])
    await_at(xs.at[my_rows], swap_send.at[1])
    for i in range(total):
        src, cols, buf, src_base, base, n = pieces[i]
        await_at(buf.at[pl.ds(0, 3), pl.ds(0, n)], piece_send.at[i])
    for i in range(2):
        await_at(pieces[i][2].at[pl.ds(0, 3), pl.ds(0, half)], core_send.at[i])
    if chips > 1:
        await_at(logs.at[pl.ds(1, chips - 1)], log_send.at[0])
    await_at(out_ref.at[:, my_cols], out_sem.at[0])
    await_at(out_ref.at[:, my_cols], give_send.at[0])
    their_cols = pl.ds(pl.multiple_of((1 - core) * nh * head_dim, LANES), nh * head_dim)
    await_at(out_ref.at[:, their_cols], give_recv.at[0])


def per_device(inputs, query_weight, key_weight, value_weight, lambda_weight, log_decay, norm_gain):
    count = lax.axis_size("ctx")
    chips = count // 2
    bits = count.bit_length() - 1
    length, width = inputs.shape[1:]
    depth, wide = value_weight.shape
    heads = log_decay.shape[2]
    levels = lambda_weight.shape[1] // heads
    state_dim = query_weight.shape[1]
    head_dim = wide // heads
    nh = heads // 2
    lams = lambda_weight.shape[1] // 2
    total = 3 + nh - 1 + LAST_PARTS + (1 if lams > CUT else 0)
    f32, bf16 = jnp.float32, jnp.bfloat16
    anywhere = pl.BlockSpec(memory_space=pl.ANY)
    dma = pltpu.SemaphoreType.DMA
    out = pl.pallas_call(
        functools.partial(fused_kernel, levels),
        out_shape=pltpu.VMEM((length, wide), bf16),
        in_specs=[anywhere] * 7,
        out_specs=anywhere,
        scratch_shapes=[
            pltpu.VMEM((1, wide), f32),
            pltpu.VMEM((2 * length, width), bf16),
            pltpu.VMEM((2 * nh, length), f32),
            pltpu.VMEM((4, depth, state_dim), bf16),
            pltpu.VMEM((4, depth, state_dim), bf16),
            pltpu.VMEM((4, lams, depth), bf16),
            pltpu.VMEM((nh, 4, depth, head_dim), bf16),
            pltpu.VMEM((2 * length, 2 * state_dim), bf16),
            pltpu.VMEM((2, 2 * length, -(-max(CUT, lams - CUT) // LANES) * LANES), f32),
            pltpu.VMEM((nh, 2 * length, head_dim), bf16),
            pltpu.VMEM((2, length, length), f32),
            pltpu.VMEM((2 * nh, length), f32),
            pltpu.VMEM((length, 2 * nh), f32),
            pltpu.VMEM((length, 2 * nh), f32),
            pltpu.VMEM((length, 2 * nh), f32),
            pltpu.VMEM((2 * nh, length), f32),
            pltpu.VMEM((state_dim, 2 * length), f32),
            pltpu.VMEM((chips, nh, LANES), f32),
            pltpu.VMEM((bits, 5, nh, LANES), f32),
            pltpu.VMEM((nh, state_dim, head_dim), f32),
            pltpu.VMEM((bits, nh, state_dim, head_dim), bf16),
            pltpu.VMEM((bits, nh, state_dim, head_dim), bf16),
            pltpu.VMEM((nh, state_dim, head_dim), bf16),
            pltpu.VMEM((nh, 2 * length, head_dim), f32),
            pltpu.VMEM((nh, 2 * length, head_dim), bf16),
            dma((7,)),
            dma((2,)),
            dma((2,)),
            dma((total,)),
            dma((total,)),
            dma((total,)),
            dma((2,)),
            dma((2,)),
            dma((1,)),
            dma((1,)),
            dma((bits,)),
            dma((bits, nh)),
            dma((2,)),
            dma((1,)),
            dma((1,)),
            dma((1,)),
            pltpu.SemaphoreType.REGULAR,
            pltpu.SemaphoreType.REGULAR,
        ],
        compiler_params=pltpu.CompilerParams(
            collective_id=0, has_side_effects=True, vmem_limit_bytes=VMEM_LIMIT),
        name="gather_mix",
    )(inputs[0], query_weight, key_weight, lambda_weight.T, value_weight, log_decay[0].T,
      norm_gain[None])
    return out[None]


def solution(mesh):
    return jax.shard_map(
        per_device,
        mesh=mesh,
        in_specs=(
            P("dp", "ctx", None),
            P("dp", None),
            P("dp", None),
            P("dp", None),
            P("dp", None),
            P("dp", "ctx", None),
            P(),
        ),
        out_specs=P("dp", "ctx", None),
        check_vma=False,
    )
```

```python
import functools
import math

import jax
import jax.numpy as jnp
from jax import lax
from jax.experimental import pallas as pl
from jax.experimental.pallas import tpu as pltpu
from jax.sharding import PartitionSpec as P

HIGHEST = lax.Precision.HIGHEST
MESH = pl.DeviceIdType.MESH
VMEM_LIMIT = 60 * 1024 * 1024

AHEAD = 2.0
SHARE = 6 / 16
SHARE_FIRST = 8 / 16
SHARE_LATE = (8 / 16,) * 4
CUT = 160
LAST_PARTS = 4
DIRECT = 1
LANES = 128


def flipped(index, mask):
    out = index
    for power in range(mask.bit_length()):
        if mask >> power & 1:
            step = 1 << power
            out = out + step - 2 * step * ((index // step) % 2)
    return out


def fused_kernel(levels, x_ref, q_ref, k_ref, lam_t_ref, v_ref, decay_ref, gain_hbm, out_ref,
                 gain_ref, xs, dec, big_q, big_k, big_l, big_v, qk, lam, val, score, cum_rows, cum_cols,
                 grow, reach_grow, remain, keys_t, logs, coef, state, sent, got, got_far, mixed, result,
                 load_sem, swap_send, swap_recv, own_recv, cross_recv, piece_send, core_send,
                 core_recv, log_send, log_recv, st_send, st_recv, direct_send, out_sem,
                 give_send, give_recv, greet_up, greet_down):
    f32, bf16 = jnp.float32, jnp.bfloat16
    count = lax.axis_size("ctx")
    chips = count // 2
    bits = count.bit_length() - 1
    dp = lax.axis_index("dp")
    ctx = lax.axis_index("ctx")
    x_at, y_at = dp % 2, dp // 2
    core = ctx % 2
    side = (ctx // 2) % 2
    length = x_ref.shape[0]
    depth, wide = v_ref.shape
    nh = decay_ref.shape[0] // 2
    lams = lam_t_ref.shape[0] // 2
    head_dim = wide // (2 * nh)
    state_dim = q_ref.shape[1]
    inner = length.bit_length()
    scale = 1.0 / math.sqrt(state_dim)
    to_x = {"dp": y_at * 2 + (1 - x_at)}
    to_y = {"dp": (1 - y_at) * 2 + x_at}
    to_core = {"ctx": flipped(ctx, 1)}
    to_z = {"ctx": flipped(ctx, 2)}
    peers = [None] + [{"ctx": flipped(ctx, 2 * r)} for r in range(1, chips)]
    owners = (y_at * 2 + (1 - x_at), (1 - y_at) * 2 + x_at, (1 - y_at) * 2 + (1 - x_at), dp)
    def remote(src, dst, out_sem_, in_sem, target):
        pltpu.make_async_remote_copy(
            src_ref=src, dst_ref=dst, send_sem=out_sem_, recv_sem=in_sem,
            device_id=target, device_id_type=MESH).start()

    def await_at(spot, sem):
        pltpu.make_async_copy(spot, spot, sem).wait()

    chip = ctx // 2
    below, above = chip > 0, chip < chips - 1
    to_below, to_above = {"ctx": (ctx + count - 2) % count}, {"ctx": (ctx + 2) % count}
    barrier = pltpu.get_barrier_semaphore()
    for target in (to_x, to_y, to_core):
        pl.semaphore_signal(barrier, inc=1, device_id=target, device_id_type=MESH)
    for there, target in ((below, to_below), (above, to_above)):
        @pl.when(there)
        def _(target=target):
            pl.semaphore_signal(barrier, inc=1, device_id=target, device_id_type=MESH)

    def greet_all():
        def pass_along(sem, first, then, target):
            @pl.when(first)
            def _():
                pl.semaphore_wait(sem, 1)

            @pl.when(then)
            def _():
                pl.semaphore_signal(sem, inc=1, device_id=target, device_id_type=MESH)

        @pl.when(chip >= chips // 2)
        def _():
            pass_along(greet_down, above, below, to_below)
        pass_along(greet_up, below, above, to_above)

        @pl.when(chip < chips // 2)
        def _():
            pass_along(greet_down, above, below, to_below)

    my_rows = pl.ds(pl.multiple_of(core * length, length), length)
    my_heads = pl.ds(pl.multiple_of(core * nh, nh), nh)
    their_heads = pl.ds(pl.multiple_of((1 - core) * nh, nh), nh)
    my_lams = pl.ds(pl.multiple_of(core * lams, 16), lams)
    my_cols = pl.ds(pl.multiple_of(core * nh * head_dim, LANES), nh * head_dim)

    def head_cols(h):
        return pl.ds(pl.multiple_of((core * nh + h) * head_dim, LANES), head_dim)

    local = [
        pltpu.make_async_copy(decay_ref.at[my_heads], dec.at[my_heads], load_sem.at[0]),
        pltpu.make_async_copy(x_ref, xs.at[my_rows], load_sem.at[1]),
        pltpu.make_async_copy(q_ref, big_q.at[3], load_sem.at[2]),
        pltpu.make_async_copy(k_ref, big_k.at[3], load_sem.at[3]),
        pltpu.make_async_copy(lam_t_ref.at[my_lams], big_l.at[3], load_sem.at[4]),
        pltpu.make_async_copy(gain_hbm, gain_ref, load_sem.at[5]),
    ] + [pltpu.make_async_copy(v_ref.at[:, head_cols(h)], big_v.at[h, 3], load_sem.at[6])
         for h in range(nh)]

    half = depth // 2
    cut = min(lams, CUT)
    lam_parts = [(0, cut)] + ([(cut, lams)] if cut < lams else [])
    pieces = [(k_ref, None, big_k, core * half, core * half, half),
              (q_ref, None, big_q, core * half, core * half, half),
              (lam_t_ref, None, big_l, core * lams, 0, cut)]
    parts = []
    for h in range(nh):
        size = depth // (LAST_PARTS if h == nh - 1 else 1)
        parts.append(range(len(pieces), len(pieces) + depth // size))
        pieces += [(v_ref, head_cols(h), big_v.at[h], low, low, size)
                   for low in range(0, depth, size)]
    pieces += [(lam_t_ref, None, big_l, core * lams + low, low, high - low)
               for low, high in lam_parts[1:]]
    total = len(pieces)
    weight = [piece[5] * (depth if piece[0] is lam_t_ref else head_dim) / (depth * head_dim)
              for piece in pieces]
    issued = []

    def send_ahead(step):
        while (len(issued) < total
               and sum(weight[step + 1:len(issued) + 1]) <= AHEAD):
            send_own(len(issued))
            issued.append(step)

    share = [SHARE_FIRST] * 5 + [SHARE] * (total - 5)
    share[total - len(SHARE_LATE):] = SHARE_LATE

    def shares(i):
        n = pieces[i][5]
        first = (n // 2 + 15) // 16 * 16
        shared = min(int(n * share[i] / 16 + 0.5) * 16, n - first)
        return shared, n - shared, first

    def rows_at(base, start, size):
        return pl.ds(pl.multiple_of(base + start, 16), size)

    def direct_start(way, shared):
        return (1 - side if way else side) * shared

    def send_own(i):
        src, cols, buf, src_base, base, n = pieces[i]
        shared, direct, first = shares(i)
        for way, target in enumerate((to_x, to_y)):
            start = direct_start(way, shared)
            rows = rows_at(src_base, start, direct)
            remote(src.at[rows] if cols is None else src.at[rows, cols],
                   buf.at[way, rows_at(base, start, direct)],
                   piece_send.at[i], own_recv.at[i], target)

    def relays(i):
        src, cols, buf, src_base, base, n = pieces[i]
        shared, direct, first = shares(i)
        return ((0, to_y, rows_at(base, side * (n - first), first)),
                (1, to_x, rows_at(base, (1 - side) * first, n - first)))

    def relay(i):
        src, cols, buf, src_base, base, n = pieces[i]
        shared, direct, first = shares(i)
        await_at(buf.at[pl.ds(0, 2), pl.ds(0, direct)], own_recv.at[i])
        for way, target, rows in relays(i):
            remote(buf.at[way, rows], buf.at[2, rows], piece_send.at[i], cross_recv.at[i], target)
        if shared > 0:
            for way in range(2):
                rows = rows_at(base, (1 - side if way else side) * direct, shared)
                remote(buf.at[way, rows], buf.at[way, rows], piece_send.at[i],
                       cross_recv.at[i], to_z)

    def crossed(i):
        src, cols, buf, src_base, base, n = pieces[i]
        shared, direct, first = shares(i)
        await_at(buf.at[pl.ds(0, 2), pl.ds(0, n // 2 + shared)], cross_recv.at[i])
        if i < 2:
            spot = buf.at[pl.ds(0, 3), rows_at(base, 0, n)]
            remote(spot, spot, core_send.at[i], core_recv.at[i], to_core)

    def own_part(way, low=0, size=depth):
        return pl.ds(pl.multiple_of(owners[way] * depth + low, LANES), size)

    plain = (((1,), (0,)), ((), ()))
    turned = (((1,), (1,)), ((), ()))

    def gathered(weights, dims, ways=(3, 0, 1, 2), acc=None):
        for way in ways:
            term = lax.dot_general(
                xs[:, own_part(way)], weights(way), dims, preferred_element_type=f32)
            acc = term if acc is None else acc + term
        return acc

    def task_k():
        await_at(big_k.at[pl.ds(0, 3), rows_at((1 - core) * half, 0, half)], core_recv.at[0])
        keys = gathered(lambda way: big_k[way], plain).astype(bf16)
        qk[:, state_dim:] = keys
        keys_t[...] = keys.astype(f32).T

    def task_q():
        await_at(big_q.at[pl.ds(0, 3), rows_at((1 - core) * half, 0, half)], core_recv.at[1])
        qk[:, :state_dim] = gathered(lambda way: big_q[way], plain).astype(bf16)
        row = lax.broadcasted_iota(jnp.int32, (length, length), 0)
        col = lax.broadcasted_iota(jnp.int32, (length, length), 1)
        for blk in range(2):
            rows = slice(blk * length, (blk + 1) * length)
            full = lax.dot_general(
                qk[rows, :state_dim], qk[rows, state_dim:], turned, preferred_element_type=f32)
            score[blk] = jnp.where(row >= col, full * scale, 0.0)

    def task_lam(part):
        low, high = lam_parts[part]
        lam[part, :, :high - low] = jax.nn.softplus(
            gathered(lambda way: big_l[way, low:high], turned))

    def lam_at(rows, at):
        part = 0 if at < cut else 1
        at -= part * cut
        return lam[part, rows, at:at + 1]

    def task_early(h):
        mixed[h] = gathered(lambda way: big_v[h, way], plain, (3,))

    def task_sums():
        row = lax.broadcasted_iota(jnp.int32, (length, length), 0)
        col = lax.broadcasted_iota(jnp.int32, (length, length), 1)
        below = (row >= col).astype(f32)
        decays = dec[...]
        ones = jnp.ones((length, LANES), f32)
        sums = jnp.dot(decays, ones, precision=HIGHEST, preferred_element_type=f32)
        logs[0] = sums[:nh] + sums[nh:]
        coef[0, 0] = jnp.exp(sums[nh:])
        for r in range(1, chips):
            remote(logs.at[0], logs.at[r], log_send.at[0], log_recv.at[0], peers[r])
        cum_col = lax.dot_general(
            below, decays, turned, precision=HIGHEST, preferred_element_type=f32)
        cum_row = lax.dot_general(
            decays, below, turned, precision=HIGHEST, preferred_element_type=f32)
        cum_rows[...] = cum_row
        moved = jnp.concatenate((jnp.zeros((nh, length), f32), decays[:nh]), axis=0)
        before = lax.dot_general(
            jnp.ones((length, length), f32), moved, turned, precision=HIGHEST,
            preferred_element_type=f32)
        cum_cols[...] = cum_col
        grow[...] = jnp.exp(cum_col) * scale
        reach_grow[...] = jnp.exp(cum_col + before) * scale
        remain[...] = jnp.exp(cum_row[:, length - 1:length] - cum_row)

    def task_coef():
        if chips > 1:
            await_at(logs.at[pl.ds(1, chips - 1)], log_recv.at[0])
        own_log = logs[0]
        carry_log = jnp.zeros_like(own_log)
        for b in range(1, bits):
            upper = ((ctx // (1 << b)) % 2).astype(f32)
            step = 1 << (b - 1)
            other = logs[step]
            for r in range(step + 1, 2 * step):
                other = other + logs[r]
            coef[b, 0] = jnp.exp(carry_log) * upper
            coef[b, 1] = jnp.where(upper > 0, 1.0, jnp.exp(other))
            coef[b, 2] = jnp.where(upper > 0, jnp.exp(own_log), 1.0)
            if b == bits - 1 and b > 1:
                same = logs[step]
                for r in range(step + 1, step + step // 2):
                    same = same + logs[r]
                odd = ((ctx // (1 << (b - 1))) % 2).astype(f32)
                late = jnp.exp(jnp.where(odd > 0, same, other - same))
                coef[b, 3] = jnp.where(odd > 0, 1.0, late)
                coef[b, 4] = jnp.where(odd > 0, late, 1.0)
            carry_log = carry_log + upper * other
            own_log = own_log + other

    def upper_at(b):
        return (ctx // (1 << b)) % 2 == 1

    def merges_at(b):
        return ctx // (2 << b) != count // (2 << b) - 1

    def state_copy(h, b):
        return pltpu.make_async_remote_copy(
            src_ref=sent.at[b, h], dst_ref=got.at[b, h], send_sem=st_send.at[b],
            recv_sem=st_recv.at[b, h], device_id=peers[1 << (b - 1)], device_id_type=MESH)

    def sends_at(b):
        return jnp.logical_or(jnp.logical_not(upper_at(b)), merges_at(b))

    def takes_at(b):
        return jnp.logical_or(upper_at(b), merges_at(b))

    top, mid = bits - 1, bits - 2

    def is_direct(h):
        return bits > 2 and h >= nh - DIRECT

    def send_direct(h):
        source = sent.at[mid, h]

        @pl.when(jnp.logical_not(upper_at(mid)))
        def _():
            remote(source, got.at[mid, h], direct_send.at[0], st_recv.at[mid, h],
                   peers[1 << (mid - 1)])

        @pl.when(jnp.logical_not(upper_at(top)))
        def _():
            remote(source, got.at[top, h], direct_send.at[1], st_recv.at[top, h],
                   peers[1 << (top - 1)])
            remote(source, got_far.at[h], direct_send.at[1], st_recv.at[top, h],
                   peers[3 << (mid - 1)])

    def send_state(h, b):
        if is_direct(h) and b == mid:
            send_direct(h)
            return

        @pl.when(sends_at(b))
        def _():
            state_copy(h, b).start()

    def await_state(h, b):
        @pl.when(takes_at(b))
        def _():
            await_at(got.at[b, h], st_recv.at[b, h])

    def add_part(h, p):
        low, size = pieces[parts[h][p]][4:]
        acc = mixed[h]
        for way in range(3):
            acc = acc + jnp.dot(
                xs[:, own_part(way, low, size)], big_v[h, way, low:low + size],
                preferred_element_type=f32)
        return acc

    def task_part(h, p):
        mixed[h] = add_part(h, p)

    def task_head(h):
        val[h] = add_part(h, len(parts[h]) - 1).astype(bf16)
        blocks = []
        for blk in range(2):
            rows = slice(blk * length, (blk + 1) * length)
            at = blk * nh + h
            keyed = (keys_t[:, rows] * remain[at:at + 1]).astype(bf16)
            blocks.append(jnp.dot(keyed, val[h, rows], preferred_element_type=f32))
        sent[0, h] = blocks[0].astype(bf16)
        if bits > 1:
            whole = coef[0, 0, h:h + 1] * blocks[0] + blocks[1]
            state[h] = whole
            sent[1, h] = whole.astype(bf16)
            send_state(h, 1)

    tile = 128
    tiles = length // tile

    def task_near(h, blk):
        trow = lax.broadcasted_iota(jnp.int32, (tile, tile), 0)
        tcol = lax.broadcasted_iota(jnp.int32, (tile, tile), 1)
        differ = jnp.bitwise_xor(trow, tcol)
        deep = tile.bit_length() - 1
        base = h * levels
        at_cum = blk * nh + h
        low = blk * length
        for ti in range(tiles):
            rows = slice(low + ti * tile, low + (ti + 1) * tile)
            here = slice(ti * tile, (ti + 1) * tile)
            acc = None
            for tj in range(ti + 1):
                cols = slice(tj * tile, (tj + 1) * tile)
                if ti == tj:
                    weight = jnp.broadcast_to(lam_at(rows, base), (tile, tile))
                    for level in range(1, deep + 1):
                        at = base + level
                        weight = jnp.where(
                            differ >= 1 << (level - 1), lam_at(rows, at), weight)
                else:
                    at = base + deep + (ti ^ tj).bit_length()
                    weight = lam_at(rows, at)
                distance = cum_cols[here, at_cum:at_cum + 1] - cum_rows[at_cum:at_cum + 1, cols]
                decay = jnp.exp(jnp.minimum(distance, 0.0))
                mix = (weight * (decay * score[blk, here, cols])).astype(bf16)
                term = jnp.dot(
                    mix, val[h, low + tj * tile:low + (tj + 1) * tile],
                    preferred_element_type=f32)
                acc = term if acc is None else acc + term
            if blk == 1:
                reach = jnp.dot(qk[rows, :state_dim], sent[0, h], preferred_element_type=f32)
                at = base + inner
                acc = acc + lam_at(rows, at) * grow[here, at_cum:at_cum + 1] * reach
            mixed[h, rows] = acc

    def far(h, b):
        other = got[b, h].astype(f32)
        if is_direct(h) and b == top:
            other = coef[b, 3, h:h + 1] * other + coef[b, 4, h:h + 1] * got_far[h].astype(f32)
        carried = (coef[b, 0, h:h + 1] * other).astype(bf16)
        reach = jnp.dot(qk[:, :state_dim], carried, preferred_element_type=f32)
        at = h * levels + inner + b
        grown = jnp.concatenate((reach_grow[:, h:h + 1], reach_grow[:, nh + h:nh + h + 1]), axis=0)
        return lam_at(slice(None), at) * grown * reach

    def task_merge(h, b):
        await_state(h, b)

        @pl.when(merges_at(b))
        def _():
            block = coef[b, 1, h:h + 1] * state[h] + coef[b, 2, h:h + 1] * got[b, h].astype(f32)
            state[h] = block
            sent[b + 1, h] = block.astype(bf16)
        send_state(h, b + 1)

    def task_far(h, b):
        @pl.when(upper_at(b))
        def _():
            if is_direct(h) and b >= mid:
                await_at(got.at[pl.ds(0, 1 + (b == top)), h], st_recv.at[b, h])
            mixed[h] += far(h, b)

    def task_finish(h):
        if bits > 1:
            if not is_direct(h):
                await_state(h, top)
            task_far(h, top)
        whole = mixed[h]
        mean_square = jnp.mean(whole * whole, axis=-1, keepdims=True)
        gain = gain_ref[:, head_cols(h)]
        result[h] = (whole * lax.rsqrt(mean_square + 1e-05) * gain).astype(bf16)
        remote(result.at[h, pl.ds(pl.multiple_of((1 - core) * length, length), length)],
               out_ref.at[:, head_cols(h)], give_send.at[0], give_recv.at[0], to_core)
        pltpu.make_async_copy(
            result.at[h, my_rows], out_ref.at[:, head_cols(h)], out_sem.at[0]).start()

    for copy in local:
        copy.start()
    pl.semaphore_wait(barrier, 3 + below.astype(jnp.int32) + above.astype(jnp.int32))
    send_ahead(-1)
    remote(decay_ref.at[their_heads], dec.at[my_heads], swap_send.at[0], swap_recv.at[0], to_core)
    remote(x_ref, xs.at[my_rows], swap_send.at[1], swap_recv.at[1], to_core)
    greet_all()

    def task_loads():
        for copy in local[1:6]:
            copy.wait()
        await_at(big_v.at[:, 3], load_sem.at[6])
        await_at(
            xs.at[pl.ds(pl.multiple_of((1 - core) * length, length), length)], swap_recv.at[1])

    def task_decays():
        local[0].wait()
        await_at(dec.at[their_heads], swap_recv.at[0])
        task_sums()

    def task_output(h):
        task_finish(h)

    def call(task, *what):
        return functools.partial(task, *what)

    tasks = {}
    final = total

    def plan(step, rank, task, *what):
        tasks.setdefault(min(step, final), []).append((rank, call(task, *what)))

    plan(1, 0, task_decays)
    plan(2, 0, task_loads)
    for h in range(nh):
        plan(2 + h // 3, 2, task_early, h)
    plan(3, 0, task_coef)
    plan(2, 1, task_k)
    plan(3, 0, task_q)
    plan(3, 1, task_lam, 0)
    for p in range(1, len(lam_parts)):
        plan(final, 2, task_lam, p)
    for h in range(nh):
        at = parts[h][-1] + 1
        left = nh - 1 - h
        for p in range(len(parts[h]) - 1):
            plan(parts[h][p] + 1, 0, task_part, h, p)
        plan(at, 1, task_head, h)
        merged = at + 1
        near = (at + 1, at + 1)
        if (h + 1) * levels > cut:
            near = (final, final)
        for b in range(1, mid if is_direct(h) else top):
            plan(merged, 3, task_merge, h, b)
        for b in range(1, top):
            plan(near[1], 8 if left == 0 else 6, task_far, h, b)
        for blk in range(2):
            plan(near[blk], 5, task_near, h, blk)
        if left > 2:
            plan(at + 2, 4, task_output, h)
        else:
            plan(final - 1 if left == 2 else final, 9 if left == 0 else 7, task_output, h)
    for step in range(total + 1):
        due = [step] if step < total - LAST_PARTS else range(step, total) if step == total - LAST_PARTS else []
        for i in due:
            relay(i)
            send_ahead(i)
        if step >= 1:
            crossed(step - 1)
        for rank, task in sorted(tasks.pop(step, []), key=lambda entry: entry[0]):
            task()
    for b in range(1, bits):
        heads_at = nh - (DIRECT if bits > 2 and b >= mid else 0)

        @pl.when(sends_at(b))
        def _(b=b, heads_at=heads_at):
            await_at(sent.at[b, pl.ds(0, heads_at)], st_send.at[b])
    if bits > 2 and DIRECT:
        @pl.when(jnp.logical_not(upper_at(mid)))
        def _():
            await_at(sent.at[0, pl.ds(0, DIRECT)], direct_send.at[0])

        @pl.when(jnp.logical_not(upper_at(top)))
        def _():
            await_at(sent.at[pl.ds(0, 2), pl.ds(0, DIRECT)], direct_send.at[1])
    await_at(dec.at[their_heads], swap_send.at[0])
    await_at(xs.at[my_rows], swap_send.at[1])
    for i in range(total):
        src, cols, buf, src_base, base, n = pieces[i]
        await_at(buf.at[pl.ds(0, 3), pl.ds(0, n)], piece_send.at[i])
    for i in range(2):
        await_at(pieces[i][2].at[pl.ds(0, 3), pl.ds(0, half)], core_send.at[i])
    if chips > 1:
        await_at(logs.at[pl.ds(1, chips - 1)], log_send.at[0])
    await_at(out_ref.at[:, my_cols], out_sem.at[0])
    await_at(out_ref.at[:, my_cols], give_send.at[0])
    their_cols = pl.ds(pl.multiple_of((1 - core) * nh * head_dim, LANES), nh * head_dim)
    await_at(out_ref.at[:, their_cols], give_recv.at[0])


def per_device(inputs, query_weight, key_weight, value_weight, lambda_weight, log_decay, norm_gain):
    count = lax.axis_size("ctx")
    chips = count // 2
    bits = count.bit_length() - 1
    length, width = inputs.shape[1:]
    depth, wide = value_weight.shape
    heads = log_decay.shape[2]
    levels = lambda_weight.shape[1] // heads
    state_dim = query_weight.shape[1]
    head_dim = wide // heads
    nh = heads // 2
    lams = lambda_weight.shape[1] // 2
    total = 3 + nh - 1 + LAST_PARTS + (1 if lams > CUT else 0)
    f32, bf16 = jnp.float32, jnp.bfloat16
    anywhere = pl.BlockSpec(memory_space=pl.ANY)
    dma = pltpu.SemaphoreType.DMA
    out = pl.pallas_call(
        functools.partial(fused_kernel, levels),
        out_shape=pltpu.VMEM((length, wide), bf16),
        in_specs=[anywhere] * 7,
        out_specs=anywhere,
        scratch_shapes=[
            pltpu.VMEM((1, wide), f32),
            pltpu.VMEM((2 * length, width), bf16),
            pltpu.VMEM((2 * nh, length), f32),
            pltpu.VMEM((4, depth, state_dim), bf16),
            pltpu.VMEM((4, depth, state_dim), bf16),
            pltpu.VMEM((4, lams, depth), bf16),
            pltpu.VMEM((nh, 4, depth, head_dim), bf16),
            pltpu.VMEM((2 * length, 2 * state_dim), bf16),
            pltpu.VMEM((2, 2 * length, -(-max(CUT, lams - CUT) // LANES) * LANES), f32),
            pltpu.VMEM((nh, 2 * length, head_dim), bf16),
            pltpu.VMEM((2, length, length), f32),
            pltpu.VMEM((2 * nh, length), f32),
            pltpu.VMEM((length, 2 * nh), f32),
            pltpu.VMEM((length, 2 * nh), f32),
            pltpu.VMEM((length, 2 * nh), f32),
            pltpu.VMEM((2 * nh, length), f32),
            pltpu.VMEM((state_dim, 2 * length), f32),
            pltpu.VMEM((chips, nh, LANES), f32),
            pltpu.VMEM((bits, 5, nh, LANES), f32),
            pltpu.VMEM((nh, state_dim, head_dim), f32),
            pltpu.VMEM((bits, nh, state_dim, head_dim), bf16),
            pltpu.VMEM((bits, nh, state_dim, head_dim), bf16),
            pltpu.VMEM((nh, state_dim, head_dim), bf16),
            pltpu.VMEM((nh, 2 * length, head_dim), f32),
            pltpu.VMEM((nh, 2 * length, head_dim), bf16),
            dma((7,)),
            dma((2,)),
            dma((2,)),
            dma((total,)),
            dma((total,)),
            dma((total,)),
            dma((2,)),
            dma((2,)),
            dma((1,)),
            dma((1,)),
            dma((bits,)),
            dma((bits, nh)),
            dma((2,)),
            dma((1,)),
            dma((1,)),
            dma((1,)),
            pltpu.SemaphoreType.REGULAR,
            pltpu.SemaphoreType.REGULAR,
        ],
        compiler_params=pltpu.CompilerParams(
            collective_id=0, has_side_effects=True, vmem_limit_bytes=VMEM_LIMIT),
        name="gather_mix",
    )(inputs[0], query_weight, key_weight, lambda_weight.T, value_weight, log_decay[0].T,
      norm_gain[None])
    return out[None]


def solution(mesh):
    return jax.shard_map(
        per_device,
        mesh=mesh,
        in_specs=(
            P("dp", "ctx", None),
            P("dp", None),
            P("dp", None),
            P("dp", None),
            P("dp", None),
            P("dp", "ctx", None),
            P(),
        ),
        out_specs=P("dp", "ctx", None),
        check_vma=False,
    )
```
